128 devices in a mesh: gx: 8 (over x, core), gy: 16 (over y, z).
Axes of the slice: x: 4, y: 4, z: 4, core: 2. Of those that a mesh axis runs over, the one named last changes fastest.
Arguments:
- off_state: float32 [5, 256, 256, 256], P(None, 'gx', 'gy'), may hold values from -0.9 to 3, as said below
- near_state: float32 [384, 5, 8, 64, 128], P(('gx', 'gy')), may hold values from -0.9 to 3, as said below
- near_metric: float32 [384, 3, 8, 64, 128], P(('gx', 'gy')), may hold values from 0.5 to 1.1
- slot_block: int32 [384], P(('gx', 'gy')), may hold values from -1 to 255, as said below
- block_faces: int32 [256, 2], replicated, may hold values from 0 to 255, as said below
- fringe_in: int32 [3, 1024], P(None, ('gx', 'gy')), may hold values from 0 to 23, as said below
- fringe_in_maps: bfloat16 [1024, 128, 128], P(('gx', 'gy')), may hold values from 0 to 1
- fringe_out: int32 [3, 1024], P(None, ('gx', 'gy')), may hold values from 0 to 23, as said below
- fringe_out_maps: bfloat16 [1024, 128, 128], P(('gx', 'gy')), may hold values from 0 to 1
Outputs:
- off_next: float32 [5, 256, 256, 256], P(None, 'gx', 'gy')
- near_next: float32 [384, 5, 8, 64, 128], P(('gx', 'gy'))
The draws below stay inside these ranges and needn't reach their ends.
Inputs may be any that keep to these rules, and one draw needn't show every extreme that they name: `off_state`: component 0 (density) lies within 0.8 to 1.2, components 1 to 3 within -0.9 to 0.9, component 4 within 2 to 3. `near_state`: component 0 (density) lies within 0.8 to 1.2, components 1 to 3 within -0.9 to 0.9, component 4 within 2 to 3, in empty slots too. `slot_block`: entry 3 * d + s is the block in slot s of device d (devices in gx+gy order). A device's occupied slots come first and it holds at least one block; every block is in exactly one slot; the blocks of gx row r are numbered from r * 2 * 16 and held in that row; the devices at gy and gy + 8 of one row hold 4 blocks together. `block_faces`: row b gives the block across b's lower and upper face around the body; they agree (b is the lower neighbour of its upper neighbour) and lie in b's gx row. `fringe_in`: column 8 * d + k is row k of device d: entry 0 a near-body tile of d in an occupied slot, entry 1 the gy index of the receiving device in d's gx row, entry 2 one of its off-body tiles. Every off-body tile is replaced at most once; every device receives exactly 8 rows, and sends exactly 1 row to each of 8 devices. `fringe_out`: column 8 * d + k is row k of device d: entry 0 an off-body tile of d, entry 1 the gy index of the receiving device in d's gx row, entry 2 a near-body tile of that device in an occupied slot. Every near-body tile is replaced at most once; every device receives exactly 8 rows, and sends exactly 1 row to each of 8 devices.
All inputs are finite; a program needn't handle non-finite values.
Results may differ from the reference program's by a relative error of at most 0.0014.
The reference program's roundings to bfloat16 on the way count: a program that leaves them out, or rounds other values in their place, can miss the bound.
Values may be sent and summed in bfloat16 or wider, within the bound.
A program may use at most 384 MiB of HBM per device.

```python
import math
import jax
import jax.numpy as jnp
from jax import lax

CX = 32
CY = 16
NZ = 256
TW = 8
TL = 128
NJ = 64
BLK_DEV = 2
FR_DEV = 8
FCAP = 1
NX = 256
NY = 256
BCAP = 3
SLOTS = 384
TPB = 8
NT_OFF = 16
N_GX = 8
N_GY = 16
DEVICES = 128


def alternating(cells):
    dimensions = len(cells)
    index_sum = jnp.zeros((), jnp.int32)
    for axis_number in range(dimensions - 3, dimensions):
        view_shape = [1] * dimensions
        view_shape[axis_number] = cells[axis_number]
        index_sum = index_sum + jnp.arange(cells[axis_number], dtype=jnp.int32).reshape(view_shape)
    return 1.0 - 2.0 * (index_sum % 2).astype(jnp.float32)


def flow_fields(key, cells):
    density_key, momentum_key, energy_key = jax.random.split(key, 3)
    lone_member = (1,) + cells
    parity_sign = alternating(cells)[None]
    density = 0.8 + 0.4 * jax.random.uniform(density_key, lone_member)
    magnitude = jax.random.uniform(momentum_key, (3,) + cells, minval=0.2, maxval=0.8)
    energy = 2.0 + jax.random.uniform(energy_key, lone_member)
    momentum = parity_sign * magnitude
    return jnp.concatenate([density, momentum, energy], axis=0).astype(jnp.float32)


def draw_off_state(key, part):
    return flow_fields(jax.random.fold_in(key, 1), (NX, NY, NZ))


def draw_near_state(key, part):
    fields = flow_fields(jax.random.fold_in(key, 2), (SLOTS, TW, NJ, TL))
    return jnp.moveaxis(fields, 0, 1)


def interpolation_maps(key, row_total):
    scores = 3.0 * jax.random.normal(key, (row_total, TL, TL))
    weights = jax.nn.softmax(scores, axis=-1)
    return (0.6 * jnp.eye(TL, dtype=jnp.float32) + 0.4 * weights).astype(jnp.bfloat16)


def draw_fringe_in_maps(key, part):
    return interpolation_maps(jax.random.fold_in(key, 3), DEVICES * FR_DEV)


def draw_fringe_out_maps(key, part):
    return interpolation_maps(jax.random.fold_in(key, 4), DEVICES * FR_DEV)


def placement(key):
    half_axis = N_GY // 2
    row_keys = jax.random.split(jax.random.fold_in(key, 11), N_GX)
    pair_load = jax.random.randint(jax.random.fold_in(key, 12), (N_GX, half_axis), 1, 2 * BLK_DEV)
    heavy_pair = jax.random.randint(jax.random.fold_in(key, 13), (N_GX, 1), 0, half_axis)
    pair_load = jnp.where(jnp.arange(half_axis)[None, :] == heavy_pair, 2 * BLK_DEV - 1, pair_load)
    row_order = jax.vmap(lambda row_key: jax.random.permutation(row_key, BLK_DEV * N_GY))(row_keys)
    column = jnp.arange(N_GY)
    pair_index = column % half_axis
    upper_half = (column >= half_axis)[None, :]
    lower_load = pair_load[:, pair_index]
    device_load = jnp.where(upper_half, 2 * BLK_DEV - lower_load, lower_load)
    first_seat = 2 * BLK_DEV * pair_index[None, :] + jnp.where(upper_half, lower_load, 0)
    seat_index = jnp.arange(BCAP)
    position = jnp.clip(first_seat[:, :, None] + seat_index[None, None, :], 0, BLK_DEV * N_GY - 1)
    local_block = jnp.take_along_axis(row_order, position.reshape(N_GX, -1), axis=1).reshape(N_GX, N_GY, BCAP)
    blocks = jnp.arange(N_GX)[:, None, None] * (BLK_DEV * N_GY) + local_block
    seats = jnp.where(seat_index[None, None, :] < device_load[:, :, None], blocks, -1)
    return (seats.astype(jnp.int32), device_load.astype(jnp.int32))


def draw_slot_block(key, part):
    seats, device_load = placement(key)
    return seats.reshape(-1)


def draw_block_faces(key, part):
    row_keys = jax.random.split(jax.random.fold_in(key, 21), N_GX)
    length = BLK_DEV * N_GY
    cycle = jax.vmap(lambda row_key: jax.random.permutation(row_key, length))(row_keys)
    successor = jnp.roll(cycle, -1, axis=1)
    predecessor = jnp.roll(cycle, 1, axis=1)
    row_base = jnp.arange(N_GX)[:, None] * length
    row_number = jnp.arange(N_GX)[:, None]
    higher = jnp.zeros((N_GX, length), jnp.int32).at[row_number, cycle].set(successor + row_base)
    lower = jnp.zeros((N_GX, length), jnp.int32).at[row_number, cycle].set(predecessor + row_base)
    return jnp.stack([lower.reshape(-1), higher.reshape(-1)], axis=1).astype(jnp.int32)


def fringe_table(key, salt, donor_count, receiver_count, pool):
    base_key = jax.random.fold_in(key, salt)
    loop_keys = jax.random.split(jax.random.fold_in(base_key, 1), N_GX)
    loop = jax.vmap(lambda row_key: jax.random.permutation(row_key, N_GY))(loop_keys)
    loop_place = jnp.argsort(loop, axis=1)
    offset_keys = jax.random.split(jax.random.fold_in(base_key, 2), N_GX)
    offsets = jax.vmap(lambda row_key: jax.random.permutation(row_key, N_GY))(offset_keys)[:, :FR_DEV // FCAP]
    step_shift = jnp.repeat(offsets, FCAP, axis=1)
    target_place = (loop_place[:, :, None] + step_shift[:, None, :]) % N_GY
    receiver = jnp.take_along_axis(loop, target_place.reshape(N_GX, -1), axis=1).reshape(N_GX, N_GY, FR_DEV)
    tile_keys = jax.random.split(jax.random.fold_in(base_key, 3), N_GX * N_GY)
    scores = jax.vmap(lambda tile_key: jax.random.permutation(tile_key, pool))(tile_keys).reshape(N_GX, N_GY, pool)
    unusable = (jnp.arange(pool)[None, None, :] >= receiver_count[:, :, None]).astype(jnp.int32)
    ranked = jnp.argsort(scores + unusable * pool, axis=2)[:, :, :FR_DEV]
    receiver_tile = jnp.take_along_axis(ranked, receiver, axis=1)
    donor_tile = jax.random.randint(jax.random.fold_in(base_key, 4), (N_GX, N_GY, FR_DEV), 0, donor_count[:, :, None])
    return jnp.stack([donor_tile.reshape(-1), receiver.reshape(-1), receiver_tile.reshape(-1)], axis=0).astype(jnp.int32)


def draw_fringe_in(key, part):
    seats, device_load = placement(key)
    every_tile = jnp.full((N_GX, N_GY), NT_OFF, jnp.int32)
    return fringe_table(key, 31, device_load * TPB, every_tile, NT_OFF)


def draw_fringe_out(key, part):
    seats, device_load = placement(key)
    every_tile = jnp.full((N_GX, N_GY), NT_OFF, jnp.int32)
    return fringe_table(key, 41, every_tile, device_load * TPB, BCAP * TPB)


def block_levels(stream_key, dims, cuts, smallest, largest):
    factor_of = 1.0
    for dim, shards_of in cuts:
        heights = jax.random.uniform(jax.random.fold_in(jax.random.fold_in(stream_key, 6), dim), (shards_of,), jnp.float32, smallest / len(cuts), largest / len(cuts))
        factor_of = factor_of * jnp.repeat(jnp.exp(heights), dims[dim] // shards_of).reshape((-1,) + (1,) * (len(dims) - 1 - dim))
    return factor_of


def setup_inputs(seed: int = 0) -> dict:
    arg_keys = jax.random.split(jax.random.key(seed), 10)
    return {
        "off_state": draw_off_state(jax.random.fold_in(arg_keys[9], 71), 0),
        "near_state": draw_near_state(jax.random.fold_in(arg_keys[9], 71), 0),
        "near_metric": jnp.clip(jnp.exp(math.log(1.1) - 0.7884574 * jax.random.uniform(arg_keys[2], (SLOTS, 3, TW, NJ, TL), jnp.float32) ** block_levels(arg_keys[2], (SLOTS, 3, TW, NJ, TL), ((0, 128),), -0.2, 0.2)), 0.5, 1.1),
        "slot_block": draw_slot_block(jax.random.fold_in(arg_keys[9], 71), 0),
        "block_faces": draw_block_faces(jax.random.fold_in(arg_keys[9], 71), 0),
        "fringe_in": draw_fringe_in(jax.random.fold_in(arg_keys[9], 71), 0),
        "fringe_in_maps": draw_fringe_in_maps(jax.random.fold_in(arg_keys[9], 71), 0),
        "fringe_out": draw_fringe_out(jax.random.fold_in(arg_keys[9], 71), 0),
        "fringe_out_maps": draw_fringe_out_maps(jax.random.fold_in(arg_keys[9], 71), 0),
    }


HEAT_RATIO = 1.4
VISCOSITY = 0.8
CONDUCTION = 1.12
TIME_STEP = 0.1
WALL_SIGN = (1.0, -1.0, -1.0, -1.0, 1.0)
QUIET_STATE = (1.0, 0.0, 0.0, 0.0, 2.5)


def shifted(values, direction, offset):
    leading = values.ndim - 3
    selector = [slice(None)] * leading
    for spatial in range(3):
        extent = values.shape[leading + spatial]
        if spatial == direction:
            selector.append(slice(1 + offset, extent - 1 + offset))
        else:
            selector.append(slice(1, extent - 1))
    return values[tuple(selector)]


def member(values, number):
    return values[..., number, :, :, :]


def residual(padded, metric):
    density = member(padded, 0)
    reciprocal_mass_per_volume = 1.0 / density
    fluid_speed_vector = [member(padded, 1 + direction) * reciprocal_mass_per_volume for direction in range(3)]
    motion_work_share = 0.5 * (fluid_speed_vector[0] * fluid_speed_vector[0] + fluid_speed_vector[1] * fluid_speed_vector[1] + fluid_speed_vector[2] * fluid_speed_vector[2])
    energy = member(padded, 4)
    normal_stress_level = (HEAT_RATIO - 1.0) * (energy - density * motion_work_share)
    thermal_level = normal_stress_level * reciprocal_mass_per_volume
    viscous_contribution = jnp.stack([fluid_speed_vector[0], fluid_speed_vector[1], fluid_speed_vector[2], motion_work_share, thermal_level], axis=-4)
    middle = shifted(viscous_contribution, 0, 0)
    summed = None
    for direction in range(3):
        momentum = member(padded, 1 + direction)
        pieces = [momentum, momentum * fluid_speed_vector[0], momentum * fluid_speed_vector[1], momentum * fluid_speed_vector[2],
                  (energy + normal_stress_level) * fluid_speed_vector[direction]]
        pieces[1 + direction] = pieces[1 + direction] + normal_stress_level
        fluxes = jnp.stack(pieces, axis=-4)
        difference = shifted(fluxes, direction, 1) - shifted(fluxes, direction, -1)
        second = shifted(viscous_contribution, direction, 1) + shifted(viscous_contribution, direction, -1) - 2.0 * middle
        viscous = jnp.stack([jnp.zeros_like(member(second, 0)), VISCOSITY * member(second, 0),
                             VISCOSITY * member(second, 1), VISCOSITY * member(second, 2),
                             VISCOSITY * member(second, 3) + CONDUCTION * member(second, 4)], axis=-4)
        if metric is None:
            contrib = viscous - 0.5 * difference
        else:
            spacing = jnp.expand_dims(member(metric, direction), -4)
            contrib = spacing * spacing * viscous - 0.5 * spacing * difference
        summed = contrib if summed is None else summed + contrib
    return summed


def runge_kutta(initial, rate_of):
    section_one = initial + TIME_STEP * rate_of(initial)
    section_two = 0.75 * initial + 0.25 * (section_one + TIME_STEP * rate_of(section_one))
    return (1.0 / 3.0) * initial + (2.0 / 3.0) * (section_two + TIME_STEP * rate_of(section_two))


def frame_near(current, ghost_low, upper_ghost_cells):
    joined = jnp.concatenate([ghost_low, current, upper_ghost_cells], axis=3)
    wall_sign = jnp.array(WALL_SIGN, jnp.float32).reshape(5, 1, 1, 1)
    joined = jnp.concatenate([joined[:, :, 0:1] * wall_sign, joined, joined[:, :, -1:]], axis=2)
    return jnp.concatenate([joined[..., 0:1], joined, joined[..., -1:]], axis=4)


def interpolate(donors, tile_maps):
    rounded = lax.optimization_barrier(donors.astype(jnp.bfloat16)).astype(jnp.float32)
    tile_lines = rounded.reshape(donors.shape[0], -1, tile_maps.shape[-1])
    mixed_rows = jnp.einsum("rkl,rlm->rkm", tile_lines, tile_maps.astype(jnp.float32),
                            precision=lax.Precision.HIGHEST)
    result = lax.optimization_barrier(mixed_rows.astype(jnp.bfloat16)).astype(jnp.float32)
    return result.reshape(donors.shape[0], -1)


def reference(off_state, near_state, near_metric, slot_block, block_faces, fringe_in, fringe_in_maps,
              fringe_out, fringe_out_maps):
    occupied = slot_block >= 0
    quiet_state = jnp.array(QUIET_STATE, jnp.float32).reshape(1, 5, 1, 1, 1)
    near_filled = jnp.where(occupied[:, None, None, None, None], near_state, quiet_state)
    tile_count = (CX // TW) * (CY // TW) * (NZ // TL)
    per_slot = NJ // TW
    tiles_off = off_state.reshape(5, N_GX, CX // TW, TW, N_GY, CY // TW, TW, NZ // TL, TL)
    tiles_off = tiles_off.transpose(1, 4, 2, 5, 7, 0, 3, 6, 8).reshape(N_GX * N_GY * tile_count, -1)
    tiles_near = near_filled.reshape(SLOTS, 5, TW, per_slot, TW, TL)
    tiles_near = tiles_near.transpose(0, 3, 1, 2, 4, 5).reshape(SLOTS * per_slot, -1)
    device = jnp.arange(N_GX * N_GY * FR_DEV, dtype=jnp.int32) // FR_DEV
    row_first = (device // N_GY) * N_GY
    donor_in = device * (BCAP * per_slot) + fringe_in[0]
    target_in = (row_first + fringe_in[1]) * tile_count + fringe_in[2]
    donor_out = device * tile_count + fringe_out[0]
    target_out = (row_first + fringe_out[1]) * (BCAP * per_slot) + fringe_out[2]
    values_in = interpolate(tiles_near[donor_in], fringe_in_maps)
    values_out = interpolate(tiles_off[donor_out], fringe_out_maps)
    tiles_off = tiles_off.at[target_in].set(values_in)
    marks_off = jnp.zeros((N_GX * N_GY * tile_count,), jnp.float32).at[target_in].set(1.0)
    tiles_near = tiles_near.at[target_out].set(values_out)
    marks_near = jnp.zeros((SLOTS * per_slot,), jnp.float32).at[target_out].set(1.0)

    off_start = tiles_off.reshape(N_GX, N_GY, CX // TW, CY // TW, NZ // TL, 5, TW, TW, TL)
    off_start = off_start.transpose(5, 0, 2, 6, 1, 3, 7, 4, 8).reshape(5, NX, NY, NZ)
    tile_grid = marks_off.reshape(N_GX, N_GY, CX // TW, CY // TW, NZ // TL).transpose(0, 2, 1, 3, 4)
    tile_grid = tile_grid[:, :, None, :, :, None, :, None]
    spread = jnp.broadcast_to(tile_grid, (N_GX, CX // TW, TW, N_GY, CY // TW, TW, NZ // TL, TL))
    hold_off = 1.0 - spread.reshape(NX, NY, NZ)

    def off_rate(fields):
        padded = jnp.pad(fields, ((0, 0), (1, 1), (1, 1), (1, 1)), mode="wrap")

        def slab_rate(position):
            return residual(lax.dynamic_slice_in_dim(padded, position * CX, CX + 2, axis=1), None)

        slab_rates = lax.map(slab_rate, jnp.arange(N_GX, dtype=jnp.int32))
        return slab_rates.transpose(1, 0, 2, 3, 4).reshape(5, NX, NY, NZ) * hold_off

    off_next = runge_kutta(off_start, off_rate)

    near_start = tiles_near.reshape(SLOTS, per_slot, 5, TW, TW, TL)
    near_start = near_start.transpose(0, 2, 3, 1, 4, 5).reshape(SLOTS, 5, TW, NJ, TL)
    hold_near = 1.0 - jnp.repeat(marks_near.reshape(SLOTS, per_slot), TW, axis=1)[:, None, None, :, None]
    row_slots = N_GY * BCAP
    row_blocks = N_GY * BLK_DEV

    def line_advance(bundle):
        fields, metric, hold_mask, block_ids, row_number = bundle
        present = block_ids >= 0
        local_block = jnp.where(present, block_ids - row_number * row_blocks, row_blocks)
        slot_of_block = jnp.zeros((row_blocks,), jnp.int32).at[local_block].set(
            jnp.arange(row_slots, dtype=jnp.int32), mode="drop")
        guarded_block = jnp.where(present, block_ids, 0)
        lower_local = jnp.clip(block_faces[guarded_block, 0] - row_number * row_blocks, 0, row_blocks - 1)
        upper_local = jnp.clip(block_faces[guarded_block, 1] - row_number * row_blocks, 0, row_blocks - 1)
        lower_slot = slot_of_block[lower_local]
        upper_slot = slot_of_block[upper_local]

        def near_rate(current):
            ghost_low = current[lower_slot, :, :, NJ - 1:NJ, :]
            upper_ghost_cells = current[upper_slot, :, :, 0:1, :]
            return residual(frame_near(current, ghost_low, upper_ghost_cells), metric) * hold_mask

        return runge_kutta(fields, near_rate)

    bundles = (near_start.reshape(N_GX, row_slots, 5, TW, NJ, TL),
               near_metric.reshape(N_GX, row_slots, 3, TW, NJ, TL),
               hold_near.reshape(N_GX, row_slots, 1, 1, NJ, 1),
               slot_block.reshape(N_GX, row_slots),
               jnp.arange(N_GX, dtype=jnp.int32))
    stepped = lax.map(line_advance, bundles).reshape(SLOTS, 5, TW, NJ, TL)
    near_next = jnp.where(occupied[:, None, None, None, None], stepped, 0.0)
    return off_next, near_next
```

```python
import functools

import jax
import jax.numpy as jnp
from jax import lax
from jax.experimental import pallas as pl
from jax.experimental.pallas import tpu as pltpu
from jax.sharding import PartitionSpec as P

MESH = pl.DeviceIdType.MESH
F32 = jnp.float32
BF16 = jnp.bfloat16

TW = 8
TL = 128
BCAP = 3
NROW = 8
NT_OFF = 16
NT_NEAR = 24
PEERS = 16
DT = 0.1
RK = ((0.0, 1.0), (0.75, 0.25), (1.0 / 3.0, 2.0 / 3.0))

TXX, TXY, TXZ, TYY, TYZ, HX, HY, VX, VY, VZ, Q, MX, MY = range(13)
XF = (MX, TXX, TXY, TXZ, HX)
YF = (MY, TXY, TYY, TYZ, HY)
VF = (VX, VY, VZ, Q)
XK = XF + VF
YK = YF + VF

S_OFF, S_NEAR, S_LO, S_HI, S_OCC = 0, 16, 40, 43, 46


def primitives(u):
    rho, mx, my, mz, en = u
    r = 1.0 / rho
    vx, vy, vz = mx * r, my * r, mz * r
    mv = mx * vx + my * vy + mz * vz
    p = 0.4 * en - 0.2 * mv
    q = r * (0.5 * mv + 1.4 * p)
    return vx, vy, vz, p, q, en + p


def x_terms(u):
    vx, vy, vz, p, q, h = primitives(u)
    mx = u[1]
    return (mx, mx * vx + p, mx * vy, mx * vz, h * vx, vx, vy, vz, q)


def y_terms(u):
    vx, vy, vz, p, q, h = primitives(u)
    my = u[2]
    return (my, my * vx, my * vy + p, my * vz, h * vy, vx, vy, vz, q)


def interp_kernel(fin, fout, off, near, maps_in, maps_out, send, buf_in, buf_out, sems):
    copies = []
    for k in range(NROW):
        t = fin[0, k]
        copies.append(
            pltpu.make_async_copy(
                near.at[t // 8, :, :, pl.ds(pl.multiple_of((t % 8) * 8, 8), 8), :],
                buf_in.at[k],
                sems.at[0, k],
            )
        )
        t = fout[0, k]
        copies.append(
            pltpu.make_async_copy(
                off.at[
                    :,
                    pl.ds((t // 4) * 8, 8),
                    pl.ds(pl.multiple_of(((t // 2) % 2) * 8, 8), 8),
                    pl.ds(pl.multiple_of((t % 2) * 128, 128), 128),
                ],
                buf_out.at[k],
                sems.at[1, k],
            )
        )
    for c in copies:
        c.start()
    for k in range(NROW):
        for d, (buf, maps, tab) in enumerate(((buf_in, maps_in, fin), (buf_out, maps_out, fout))):
            copies[2 * k + d].wait()
            x = buf[k].reshape(320, 128).astype(BF16)
            y = jnp.dot(x, maps[k], preferred_element_type=F32)
            send[d, tab[1, k]] = y.astype(BF16)


def interpolate(fringe_in, fringe_out, off_state, near_state, maps_in, maps_out):
    return pl.pallas_call(
        interp_kernel,
        out_shape=jax.ShapeDtypeStruct((2, PEERS, 320, 128), BF16),
        in_specs=[
            pl.BlockSpec(memory_space=pltpu.SMEM),
            pl.BlockSpec(memory_space=pltpu.SMEM),
            pl.BlockSpec(memory_space=pl.ANY),
            pl.BlockSpec(memory_space=pl.ANY),
            pl.BlockSpec(memory_space=pltpu.VMEM),
            pl.BlockSpec(memory_space=pltpu.VMEM),
        ],
        out_specs=pl.BlockSpec(memory_space=pltpu.VMEM),
        scratch_shapes=[
            pltpu.VMEM((NROW, 5, 8, 8, 128), F32),
            pltpu.VMEM((NROW, 5, 8, 8, 128), F32),
            pltpu.SemaphoreType.DMA((2, NROW)),
        ],
        compiler_params=pltpu.CompilerParams(vmem_limit_bytes=24 << 20),
        name="interp",
    )(fringe_in, fringe_out, off_state, near_state, maps_in, maps_out)


def main_kernel(
    tab,
    off,
    near,
    metric,
    send,
    zoff,
    znear,
    off_out,
    near_out,
    u0o,
    u0n,
    uo,
    un,
    met,
    so,
    sn,
    rzo,
    rzn,
    recv,
    fsend,
    frecv0,
    frecv1,
    frecv2,
    xrecv,
    ysend,
    yrecv,
    go,
    gn,
    load_sem,
    out_sem,
    fr_send,
    fr_recv,
    fc_send,
    fc_recv,
    hx_send,
    hx_recv,
    hy_send,
    hy_recv,
):
    frecv = (frecv0, frecv1, frecv2)
    gx = lax.axis_index("gx")
    gy = lax.axis_index("gy")
    nx = 8
    peers = [lax.rem(gy + d, PEERS) for d in range(1, PEERS)]
    xup, xdn = lax.rem(gx + 1, nx), lax.rem(gx + nx - 1, nx)
    yup, ydn = lax.rem(gy + 1, PEERS), lax.rem(gy + PEERS - 1, PEERS)

    loads = [
        pltpu.make_async_copy(off.at[:, :, pl.ds(0, 128)], u0o.at[0], load_sem.at[0]),
        pltpu.make_async_copy(off.at[:, :, pl.ds(128, 128)], u0o.at[1], load_sem.at[1]),
        pltpu.make_async_copy(near, u0n, load_sem.at[2]),
        pltpu.make_async_copy(metric, met, load_sem.at[3]),
    ]
    for c in loads:
        c.start()

    barrier = pltpu.get_barrier_semaphore()
    for p in peers:
        pl.semaphore_signal(barrier, inc=1, device_id=(gx, p), device_id_type=MESH)
    for p in (xup, xdn):
        pl.semaphore_signal(barrier, inc=1, device_id=(p, gy), device_id_type=MESH)
    pl.semaphore_wait(barrier, PEERS + 1)

    fringe = []
    for d in range(2):
        for i, p in enumerate(peers):
            fringe.append(
                pltpu.make_async_remote_copy(
                    send.at[d, p],
                    recv.at[d, gy],
                    fr_send.at[d, i],
                    fr_recv.at[d, i],
                    device_id=(gx, p),
                    device_id_type=MESH,
                )
            )
    own = [
        pltpu.make_async_copy(send.at[d, gy], recv.at[d, gy], fr_send.at[d, PEERS - 1])
        for d in range(2)
    ]
    for c in own + fringe:
        c.start()
    for c in loads:
        c.wait()
    for c in own:
        c.wait()
    for c in fringe:
        c.wait_send()
        c.wait_recv()

    def settle_off(t, _):
        src = tab[S_OFF + t]
        take = src >= 0
        at = jnp.maximum(src, 0)
        half = lax.rem(t, 2)
        base = (t // 4) * 128 + lax.rem(t // 2, 2) * 8
        for c in range(5):
            for a in range(4):
                v = recv[0, at, pl.ds(c * 64 + a * 16, 16), :].astype(F32)
                for b in range(2):
                    rows = pl.ds(pl.multiple_of(base + (2 * a + b) * 16, 8), 8)
                    old = u0o[half, c, rows, :]
                    u0o[half, c, rows, :] = jnp.where(take, v[8 * b : 8 * b + 8], old)
        return 0

    def settle_near(t, _):
        src = tab[S_NEAR + t]
        take = src >= 0
        at = jnp.maximum(src, 0)
        s = t // 8
        base = lax.rem(t, 8) * 8
        for c in range(5):
            for a in range(4):
                v = recv[1, at, pl.ds(c * 64 + a * 16, 16), :].astype(F32)
                for b in range(2):
                    rows = pl.ds(pl.multiple_of(base + (2 * a + b) * 64, 8), 8)
                    old = u0n[s, c, rows, :]
                    u0n[s, c, rows, :] = jnp.where(take, v[8 * b : 8 * b + 8], old)
        return 0

    lax.fori_loop(0, NT_OFF, settle_off, 0)
    lax.fori_loop(0, NT_NEAR, settle_near, 0)

    def halo_copies(st, u):
        return (
            pltpu.make_async_remote_copy(
                u.at[:, :, pl.ds(0, 16), :], xrecv.at[st, 1], hx_send.at[st, 0], hx_recv.at[st, 1],
                device_id=(xdn, gy), device_id_type=MESH,
            ),
            pltpu.make_async_remote_copy(
                u.at[:, :, pl.ds(496, 16), :], xrecv.at[st, 0], hx_send.at[st, 1], hx_recv.at[st, 0],
                device_id=(xup, gy), device_id_type=MESH,
            ),
            pltpu.make_async_remote_copy(
                ysend.at[st, 0], yrecv.at[st, 1], hy_send.at[st, 0], hy_recv.at[st, 1],
                device_id=(gx, ydn), device_id_type=MESH,
            ),
            pltpu.make_async_remote_copy(
                ysend.at[st, 1], yrecv.at[st, 0], hy_send.at[st, 1], hy_recv.at[st, 0],
                device_id=(gx, yup), device_id_type=MESH,
            ),
        )

    def send_halos(st, u):
        for h in range(2):
            for c in range(5):
                for side, first in ((0, 0), (1, 15)):
                    for part in range(2):
                        lo = u[h, c, pl.ds(first + part * 256, 8, stride=16), :]
                        hi = u[h, c, pl.ds(first + part * 256 + 128, 8, stride=16), :]
                        ysend[st, side, h, c, pl.ds(part * 16, 16), :] = jnp.concatenate(
                            [lo, hi], axis=0
                        ).astype(BF16)
        copies = halo_copies(st, u)
        for c in copies:
            c.start()

    def face_copies(st):
        remote = [
            pltpu.make_async_remote_copy(
                fsend.at[st], frecv[st].at[gy], fc_send.at[st, i], fc_recv.at[st, i],
                device_id=(gx, p), device_id_type=MESH,
            )
            for i, p in enumerate(peers)
        ]
        mine = pltpu.make_async_copy(fsend.at[st], frecv[st].at[gy], fc_send.at[st, PEERS - 1])
        return remote, mine

    def send_faces(st, u):
        for s in range(BCAP):
            for c in range(5):
                lo = u[s, c, pl.ds(0, 8, stride=64), :]
                hi = u[s, c, pl.ds(63, 8, stride=64), :]
                fsend[st, s, c] = jnp.concatenate([lo, hi], axis=0).astype(BF16)
        remote, mine = face_copies(st)
        for c in remote:
            c.start()
        mine.start()

    def off_p(u):
        def body(x, _):
            rows = pl.ds(pl.multiple_of(x * 16, 16), 16)
            w = [jnp.concatenate([u[0, c, rows, :], u[1, c, rows, :]], axis=1) for c in range(5)]
            rho, mx, my, mz, en = w
            vx, vy, vz, p, q, h = primitives(w)
            txz, tyz = mx * vz, my * vz
            vals = {
                TXX: mx * vx + p, TXY: mx * vy, TXZ: txz, TYY: my * vy + p, TYZ: tyz,
                HX: h * vx, HY: h * vy, VX: vx, VY: vy, VZ: vz, Q: q, MX: mx, MY: my,
            }
            for k, v in vals.items():
                so[k, 0, x + 1, pl.ds(8, 16), :] = v[:, :128]
                so[k, 1, x + 1, pl.ds(8, 16), :] = v[:, 128:]
            flux = jnp.concatenate([mz, txz, tyz, mz * vz + p, h * vz], axis=0).astype(BF16)
            visc = jnp.concatenate([vx, vy, vz, q], axis=0) * 1.6
            df = jnp.dot(flux, zoff[0], preferred_element_type=F32)
            sf = jnp.dot(visc.astype(BF16), zoff[1], preferred_element_type=F32)
            for c in range(5):
                r = df[16 * c : 16 * c + 16]
                if c:
                    r = r + sf[16 * c - 16 : 16 * c]
                rzo[0, c, rows, :] = r[:, :128]
                rzo[1, c, rows, :] = r[:, 128:]
            return 0

        lax.fori_loop(0, 32, body, 0)

    def off_ghosts(st):
        for side, plane in ((0, 0), (1, 33)):
            for h in range(2):
                w = [xrecv[st, side, h, c] for c in range(5)]
                for k, v in zip(XK, x_terms(w)):
                    so[k, h, plane, pl.ds(8, 16), :] = v
            for h in range(2):
                w = [yrecv[st, side, h, c].astype(F32) for c in range(5)]
                for i, v in enumerate(y_terms(w)):
                    go[i, side, h] = v

    def off_r(u, a, b):
        first = lax.broadcasted_iota(jnp.int32, (8, 128), 0) == 0
        last = lax.broadcasted_iota(jnp.int32, (8, 128), 0) == 7

        def body(x, _):
            for h in range(2):
                for g in range(2):
                    mid = pl.ds(8 + 8 * g, 8)
                    rows = pl.ds(pl.multiple_of(x * 16 + 8 * g, 8), 8)
                    t = (x // 8) * 4 + g * 2 + h
                    ch = jnp.where(tab[S_OFF + t] >= 0, 0.0, DT * b)
                    yl, yh = [], []
                    for i, k in enumerate(YK):
                        l = so[k, h, x + 1, pl.ds(7 + 8 * g, 8), :]
                        r = so[k, h, x + 1, pl.ds(9 + 8 * g, 8), :]
                        if g == 0:
                            e = jnp.broadcast_to(go[i, 0, h, pl.ds(x, 1), :], (8, 128))
                            l = jnp.where(first, e, l)
                        else:
                            e = jnp.broadcast_to(go[i, 1, h, pl.ds(x, 1), :], (8, 128))
                            r = jnp.where(last, e, r)
                        yl.append(l)
                        yh.append(r)
                    for c in range(5):
                        d = so[XF[c], h, x + 2, mid, :] - so[XF[c], h, x, mid, :]
                        d = d + (yh[c] - yl[c])
                        r = rzo[h, c, rows, :] - 0.5 * d
                        if c:
                            k = VF[c - 1]
                            s = so[k, h, x + 2, mid, :] + so[k, h, x, mid, :]
                            s = s + (yh[4 + c] + yl[4 + c])
                            r = r + (0.8 * s - 3.2 * so[k, h, x + 1, mid, :])
                        v = ch * r + (u[h, c, rows, :] if b == 1.0 else b * u[h, c, rows, :])
                        if a:
                            v = v + a * u0o[h, c, rows, :]
                        uo[h, c, rows, :] = v
            return 0

        lax.fori_loop(0, 32, body, 0)

    def near_p(u):
        def body(i, _):
            s = i // 8
            n = lax.rem(i, 8)
            for ch in range(4):
                rows = pl.ds(pl.multiple_of(n * 64 + ch * 16, 16), 16)
                w = [u[s, c, rows, :] for c in range(5)]
                rho, mx, my, mz, en = w
                vx, vy, vz, p, q, h = primitives(w)
                txz, tyz = mx * vz, my * vz
                vals = {
                    TXX: mx * vx + p, TXY: mx * vy, TXZ: txz, TYY: my * vy + p, TYZ: tyz,
                    HX: h * vx, HY: h * vy, VX: vx, VY: vy, VZ: vz, Q: q, MX: mx, MY: my,
                }
                for k, v in vals.items():
                    sn[k, s, n, pl.ds(8 + ch * 16, 16), :] = v
                flux = jnp.concatenate([mz, txz, tyz, mz * vz + p, h * vz], axis=0).astype(BF16)
                visc = jnp.concatenate([vx, vy, vz, q], axis=0).astype(BF16)
                df = jnp.dot(flux, znear[0], preferred_element_type=F32)
                sf = jnp.dot(visc, znear[1], preferred_element_type=F32)
                gz = met[s, 2, rows, :]
                gz2 = 0.8 * gz * gz
                for c in range(5):
                    r = gz * df[16 * c : 16 * c + 16]
                    if c:
                        r = r + gz2 * sf[16 * c - 16 : 16 * c]
                    rzn[s, c, rows, :] = r
            return 0

        lax.fori_loop(0, 8 * BCAP, body, 0)

    def near_ghosts(st):
        for s in range(BCAP):
            for side, base, part in ((0, S_LO, 8), (1, S_HI, 0)):
                at = tab[base + s]
                w = [
                    frecv[st][at // 3, lax.rem(at, 3), c].astype(F32)[part : part + 8]
                    for c in range(5)
                ]
                for i, v in enumerate(y_terms(w)):
                    gn[i, side, s] = v

    def near_r(u, a, b, final):
        first = lax.broadcasted_iota(jnp.int32, (8, 128), 0) == 0
        last = lax.broadcasted_iota(jnp.int32, (8, 128), 0) == 7

        def slot(s):
            keep = tab[S_OCC + s] > 0

            def body(n, _):
                nm = jnp.maximum(n - 1, 0)
                np_ = jnp.minimum(n + 1, 7)
                sign = jnp.where(n == 0, -1.0, 1.0)
                for qd in range(8):
                    mid = pl.ds(8 + 8 * qd, 8)
                    rows = pl.ds(pl.multiple_of(n * 64 + 8 * qd, 8), 8)
                    ch = jnp.where(tab[S_NEAR + s * 8 + qd] >= 0, 0.0, DT * b)
                    gxm, gym = met[s, 0, rows, :], met[s, 1, rows, :]
                    hx, hy = -0.5 * gxm, -0.5 * gym
                    gx2, gy2 = 0.8 * gxm * gxm, 0.8 * gym * gym
                    yl, yh = [], []
                    for i, k in enumerate(YK):
                        l = sn[k, s, n, pl.ds(7 + 8 * qd, 8), :]
                        r = sn[k, s, n, pl.ds(9 + 8 * qd, 8), :]
                        if qd == 0:
                            e = jnp.broadcast_to(gn[i, 0, s, pl.ds(n, 1), :], (8, 128))
                            l = jnp.where(first, e, l)
                        if qd == 7:
                            e = jnp.broadcast_to(gn[i, 1, s, pl.ds(n, 1), :], (8, 128))
                            r = jnp.where(last, e, r)
                        yl.append(l)
                        yh.append(r)
                    for c in range(5):
                        lo = sn[XF[c], s, nm, mid, :]
                        if c in (0, 4):
                            lo = sign * lo
                        r = rzn[s, c, rows, :] + hx * (sn[XF[c], s, np_, mid, :] - lo)
                        r = r + hy * (yh[c] - yl[c])
                        if c:
                            k = VF[c - 1]
                            f2 = sn[k, s, n, mid, :]
                            f2 = f2 + f2
                            lo = sn[k, s, nm, mid, :]
                            if c < 4:
                                lo = sign * lo
                            r = r + gx2 * (sn[k, s, np_, mid, :] + lo - f2)
                            r = r + gy2 * (yh[4 + c] + yl[4 + c] - f2)
                        v = ch * r + (u[s, c, rows, :] if b == 1.0 else b * u[s, c, rows, :])
                        if a:
                            v = v + a * u0n[s, c, rows, :]
                        if final:
                            v = jnp.where(keep, v, 0.0)
                        un[s, c, rows, :] = v
                return 0

            lax.fori_loop(0, 8, body, 0)

        outs = []
        for s in range(BCAP):
            slot(s)
            if final:
                outs.append(pltpu.make_async_copy(un.at[s], near_out.at[s], out_sem.at[2 + s]))
                outs[-1].start()
        return outs

    send_halos(0, u0o)
    send_faces(0, u0n)
    for st in range(3):
        a, b = RK[st]
        uoff = uo if st else u0o
        unear = un if st else u0n
        off_p(uoff)
        near_p(unear)
        for c in halo_copies(st, uoff):
            c.wait_send()
            c.wait_recv()
        off_ghosts(st)
        off_r(uoff, a, b)
        if st < 2:
            send_halos(st + 1, uo)
        else:
            oc = [
                pltpu.make_async_copy(uo.at[h], off_out.at[:, :, pl.ds(128 * h, 128)], out_sem.at[h])
                for h in range(2)
            ]
            for c in oc:
                c.start()
        remote, mine = face_copies(st)
        mine.wait()
        for c in remote:
            c.wait_send()
            c.wait_recv()
        near_ghosts(st)
        outs = near_r(unear, a, b, st == 2)
        if st < 2:
            send_faces(st + 1, un)
    for c in oc + outs:
        c.wait()


def advance(tab, off, near, metric, send, zoff, znear):
    return pl.pallas_call(
        main_kernel,
        out_shape=(
            jax.ShapeDtypeStruct((5, 512, 256), F32),
            jax.ShapeDtypeStruct((BCAP, 5, 512, 128), F32),
        ),
        in_specs=[pl.BlockSpec(memory_space=pltpu.SMEM)]
        + [pl.BlockSpec(memory_space=pl.ANY)] * 4
        + [pl.BlockSpec(memory_space=pltpu.VMEM)] * 2,
        out_specs=(pl.BlockSpec(memory_space=pl.ANY), pl.BlockSpec(memory_space=pl.ANY)),
        scratch_shapes=[
            pltpu.VMEM((2, 5, 512, 128), F32),
            pltpu.VMEM((BCAP, 5, 512, 128), F32),
            pltpu.VMEM((2, 5, 512, 128), F32),
            pltpu.VMEM((BCAP, 5, 512, 128), F32),
            pltpu.VMEM((BCAP, 3, 512, 128), F32),
            pltpu.VMEM((13, 2, 34, 32, 128), F32),
            pltpu.VMEM((13, BCAP, 8, 80, 128), F32),
            pltpu.VMEM((2, 5, 512, 128), F32),
            pltpu.VMEM((BCAP, 5, 512, 128), F32),
            pltpu.VMEM((2, PEERS, 320, 128), BF16),
            pltpu.VMEM((3, BCAP, 5, 16, 128), BF16),
            pltpu.VMEM((PEERS, BCAP, 5, 16, 128), BF16),
            pltpu.VMEM((PEERS, BCAP, 5, 16, 128), BF16),
            pltpu.VMEM((PEERS, BCAP, 5, 16, 128), BF16),
            pltpu.VMEM((3, 2, 2, 5, 16, 128), F32),
            pltpu.VMEM((3, 2, 2, 5, 32, 128), BF16),
            pltpu.VMEM((3, 2, 2, 5, 32, 128), BF16),
            pltpu.VMEM((9, 2, 2, 32, 128), F32),
            pltpu.VMEM((9, 2, BCAP, 8, 128), F32),
            pltpu.SemaphoreType.DMA((4,)),
            pltpu.SemaphoreType.DMA((5,)),
            pltpu.SemaphoreType.DMA((2, PEERS)),
            pltpu.SemaphoreType.DMA((2, PEERS)),
            pltpu.SemaphoreType.DMA((3, PEERS)),
            pltpu.SemaphoreType.DMA((3, PEERS)),
            pltpu.SemaphoreType.DMA((3, 2)),
            pltpu.SemaphoreType.DMA((3, 2)),
            pltpu.SemaphoreType.DMA((3, 2)),
            pltpu.SemaphoreType.DMA((3, 2)),
        ],
        compiler_params=pltpu.CompilerParams(
            collective_id=0, has_side_effects=True, vmem_limit_bytes=67043328
        ),
        name="advance",
    )(tab, off, near, metric, send, zoff, znear)


def z_matrices(width, wrap):
    row = lax.broadcasted_iota(jnp.int32, (width, width), 0)
    col = lax.broadcasted_iota(jnp.int32, (width, width), 1)
    if wrap:
        up, down = (col + 1) % width, (col + width - 1) % width
    else:
        up, down = jnp.minimum(col + 1, width - 1), jnp.maximum(col - 1, 0)
    above = (row == up).astype(F32)
    below = (row == down).astype(F32)
    centre = (row == col).astype(F32)
    scale = 0.5 if wrap else 1.0
    first = -0.5 * (above - below)
    second = scale * (above + below - 2.0 * centre)
    return jnp.stack([first, second]).astype(BF16)


def local(
    off_state,
    near_state,
    near_metric,
    slot_block,
    block_faces,
    fringe_in,
    fringe_in_maps,
    fringe_out,
    fringe_out_maps,
):
    rows = jnp.arange(PEERS, dtype=jnp.int32)

    def labels(table):
        hit = table[1][None, :] == rows[:, None]
        return jnp.sum(jnp.where(hit, table[2][None, :] + 1, 0), axis=1) - 1

    mine = jnp.concatenate(
        [
            labels(fringe_in)[:, None],
            labels(fringe_out)[:, None],
            jnp.broadcast_to(slot_block[None, :], (PEERS, BCAP)),
        ],
        axis=1,
    )
    theirs = lax.all_to_all(mine, "gy", split_axis=0, concat_axis=0, tiled=True)

    def sources(column, count):
        hit = column[None, :] == jnp.arange(count, dtype=jnp.int32)[:, None]
        return jnp.sum(jnp.where(hit, rows[None, :] + 1, 0), axis=1) - 1

    held = theirs[:, 2:].reshape(-1)
    faces = block_faces[jnp.maximum(slot_block, 0)]
    where_at = jnp.arange(PEERS * BCAP, dtype=jnp.int32)

    def position(ids):
        return jnp.sum(jnp.where(held[None, :] == ids[:, None], where_at[None, :], 0), axis=1)

    tab = jnp.concatenate(
        [
            sources(theirs[:, 0], NT_OFF),
            sources(theirs[:, 1], NT_NEAR),
            position(faces[:, 0]),
            position(faces[:, 1]),
            (slot_block >= 0).astype(jnp.int32),
        ]
    ).astype(jnp.int32)
    send = interpolate(
        fringe_in, fringe_out, off_state, near_state, fringe_in_maps, fringe_out_maps
    )
    off_next, near_next = advance(
        tab,
        off_state.reshape(5, 512, 256),
        near_state.reshape(BCAP, 5, 512, 128),
        near_metric.reshape(BCAP, 3, 512, 128),
        send,
        z_matrices(256, True),
        z_matrices(128, False),
    )
    return off_next.reshape(off_state.shape), near_next.reshape(near_state.shape)


def solution(mesh):
    in_specs = (
        P(None, "gx", "gy", None),
        P(("gx", "gy"), None, None, None, None),
        P(("gx", "gy"), None, None, None, None),
        P(("gx", "gy")),
        P(),
        P(None, ("gx", "gy")),
        P(("gx", "gy"), None, None),
        P(None, ("gx", "gy")),
        P(("gx", "gy"), None, None),
    )
    out_specs = (P(None, "gx", "gy", None), P(("gx", "gy"), None, None, None, None))
    return jax.shard_map(local, mesh=mesh, in_specs=in_specs, out_specs=out_specs, check_vma=False)
```

```python
import jax
import jax.numpy as jnp
import numpy as np
from jax import lax
from jax.experimental import pallas as pl
from jax.experimental.pallas import tpu as pltpu
from jax.sharding import PartitionSpec as P

MESH = pl.DeviceIdType.MESH
F32 = jnp.float32
BF16 = jnp.bfloat16

TW = 8
TL = 128
BCAP = 3
NROW = 8
NT_OFF = 16
NT_NEAR = 24
PEERS = 16
DT = 0.1
RK = ((0.0, 1.0), (0.75, 0.25), (1.0 / 3.0, 2.0 / 3.0))

TXX, TXY, TXZ, TYY, TYZ, HX, HY, VX, VY, VZ, Q, MX, MY = range(13)
XF = (MX, TXX, TXY, TXZ, HX)
YF = (MY, TXY, TYY, TYZ, HY)
VF = (VX, VY, VZ, Q)
XK = XF + VF
YK = YF + VF

S_OFF, S_NEAR, S_LO, S_HI, S_OCC = 0, 16, 40, 43, 46


def primitives(u):
    rho, mx, my, mz, en = u
    r = 1.0 / rho
    vx, vy, vz = mx * r, my * r, mz * r
    mv = mx * vx + my * vy + mz * vz
    p = 0.4 * en - 0.2 * mv
    q = r * (0.5 * mv + 1.4 * p)
    return vx, vy, vz, p, q, en + p


def x_terms(u):
    vx, vy, vz, p, q, h = primitives(u)
    mx = u[1]
    return (mx, mx * vx + p, mx * vy, mx * vz, h * vx, vx, vy, vz, q)


def y_terms(u):
    vx, vy, vz, p, q, h = primitives(u)
    my = u[2]
    return (my, my * vx, my * vy + p, my * vz, h * vy, vx, vy, vz, q)


OFFSETS = [((2 + i // 4) % 4, (2 + i % 4) % 4) for i in range(16)]
REMOTE = [i for i in range(16) if OFFSETS[i] != (0, 0)]
SELF = OFFSETS.index((0, 0))


def main_kernel(
    fin,
    fout,
    slot,
    faces,
    off,
    near,
    metric,
    maps_in_hbm,
    maps_out_hbm,
    zoff_hbm,
    znear_hbm,
    off_out,
    near_out,
    u0o,
    u0n,
    uo,
    un,
    met,
    so,
    sn,
    rzo,
    rzn,
    maps_in,
    maps_out,
    zoff,
    znear,
    send_in,
    send_out,
    recv_in,
    recv_out,
    tsend,
    trecv,
    fsend,
    frecv0,
    frecv1,
    frecv2,
    xrecv,
    ysend,
    yrecv,
    go,
    gn,
    ts,
    tab,
    load_sem,
    out_sem,
    t_send,
    t_recv,
    fr_send,
    fr_recv,
    fc_send,
    fc_recv,
    hx_send,
    hx_recv,
    hy_send,
    hy_recv,
):
    frecv = (frecv0, frecv1, frecv2)
    gx = lax.axis_index("gx")
    gy = lax.axis_index("gy")
    nx = 8
    yy, zz = gy // 4, lax.rem(gy, 4)

    def at(dy, dz):
        return lax.rem(yy + dy, 4) * 4 + lax.rem(zz + dz, 4)

    peers = [at(*OFFSETS[i]) for i in REMOTE]
    xup, xdn = lax.rem(gx + 1, nx), lax.rem(gx + nx - 1, nx)
    yup, ydn = lax.rem(gy + 1, PEERS), lax.rem(gy + PEERS - 1, PEERS)

    loads = [
        pltpu.make_async_copy(near, u0n, load_sem.at[0]),
        pltpu.make_async_copy(maps_in_hbm, maps_in, load_sem.at[1]),
        pltpu.make_async_copy(off.at[:, :, pl.ds(0, 128)], u0o.at[0], load_sem.at[2]),
        pltpu.make_async_copy(off.at[:, :, pl.ds(128, 128)], u0o.at[1], load_sem.at[3]),
        pltpu.make_async_copy(maps_out_hbm, maps_out, load_sem.at[4]),
        pltpu.make_async_copy(zoff_hbm, zoff, load_sem.at[5]),
        pltpu.make_async_copy(znear_hbm, znear, load_sem.at[6]),
        pltpu.make_async_copy(metric, met, load_sem.at[7]),
    ]
    for c in loads:
        c.start()

    barrier = pltpu.get_barrier_semaphore()
    for p in peers:
        pl.semaphore_signal(barrier, inc=1, device_id=(gx, p), device_id_type=MESH)
    for p in (xup, xdn):
        pl.semaphore_signal(barrier, inc=1, device_id=(p, gy), device_id_type=MESH)

    lane = lax.broadcasted_iota(jnp.int32, (8, 128), 1)
    table = jnp.full((8, 128), -1, jnp.int32)
    for k in range(NROW):
        table = jnp.where(lane == fin[1, k], fin[2, k], table)
        table = jnp.where(lane == 16 + fout[1, k], fout[2, k], table)
    for s in range(BCAP):
        table = jnp.where(lane == 32 + s, slot[s], table)
    tsend[...] = table

    def interpolate(d, first):
        rows_of, maps, out = ((fin, maps_in, send_in), (fout, maps_out, send_out))[d]

        def body(i, _):
            dest = at(2 + i // 4, 2 + lax.rem(i, 4))
            k = jnp.int32(0)
            for r in range(1, NROW):
                k = jnp.where(rows_of[1, r] == dest, r, k)
            t = rows_of[0, k]
            pieces = []
            for c in range(5):
                for n in range(8):
                    if d == 0:
                        at_row = lax.rem(t, 8) * 8 + n * 64
                        pieces.append(u0n[lax.div(t, 8), c, pl.ds(at_row, 8), :])
                    else:
                        at_row = lax.div(t, 4) * 128 + lax.rem(lax.div(t, 2), 2) * 8 + n * 16
                        pieces.append(u0o[lax.rem(t, 2), c, pl.ds(at_row, 8), :])
            x = jnp.concatenate(pieces, axis=0).astype(BF16)
            out[i] = jnp.dot(x, maps[k], preferred_element_type=F32).astype(BF16)
            return 0

        lax.fori_loop(first, first + 4, body, 0)

    def direct(d, i):
        src = (send_in, send_out)[d].at[i]
        dst = (recv_in, recv_out)[d].at[gy]
        if i == SELF:
            return pltpu.make_async_copy(src, dst, fr_send.at[d, i])
        return pltpu.make_async_remote_copy(
            src, dst, fr_send.at[d, i], fr_recv.at[d, i],
            device_id=(gx, at(*OFFSETS[i])), device_id_type=MESH,
        )

    def start_rows(d, first):
        for i in range(first, first + 4):
            direct(d, i).start()

    def finish_rows(d):
        for i in range(16):
            c = direct(d, i)
            if i == SELF:
                c.wait()
            else:
                c.wait_send()
                c.wait_recv()

    loads[0].wait()
    loads[1].wait()
    interpolate(0, 0)
    pl.semaphore_wait(barrier, PEERS + 1)
    tables = [
        pltpu.make_async_remote_copy(
            tsend, trecv.at[gy], t_send.at[i], t_recv.at[i], device_id=(gx, p), device_id_type=MESH
        )
        for i, p in enumerate(peers)
    ]
    own_table = pltpu.make_async_copy(tsend, trecv.at[gy], t_send.at[PEERS - 1])
    for c in tables:
        c.start()
    own_table.start()
    interpolate(0, 4)
    start_rows(0, 0)
    interpolate(0, 8)
    start_rows(0, 4)
    interpolate(0, 12)
    start_rows(0, 8)
    for c in loads[2:5]:
        c.wait()
    interpolate(1, 0)
    start_rows(0, 12)
    interpolate(1, 4)
    interpolate(1, 8)
    interpolate(1, 12)

    own_table.wait()
    for c in tables:
        c.wait_send()
        c.wait_recv()
    to_scalar = pltpu.make_async_copy(trecv, ts, load_sem.at[8])
    to_scalar.start()
    to_scalar.wait()

    def find_off(t, _):
        src = jnp.int32(-1)
        for g in range(PEERS):
            src = jnp.where(ts[g, 0, gy] == t, g, src)
        tab[S_OFF + t] = src
        return 0

    def find_near(t, _):
        src = jnp.int32(-1)
        for g in range(PEERS):
            src = jnp.where(ts[g, 0, 16 + gy] == t, g, src)
        tab[S_NEAR + t] = src
        return 0

    lax.fori_loop(0, NT_OFF, find_off, 0)
    lax.fori_loop(0, NT_NEAR, find_near, 0)
    for s in range(BCAP):
        tab[S_OCC + s] = jnp.where(slot[s] >= 0, 1, 0)
        block = jnp.maximum(slot[s], 0)
        low, high = faces[0, block], faces[1, block]

        def find_face(g, pos):
            for e in range(BCAP):
                held = ts[g, 0, 32 + e]
                pos = (
                    jnp.where(held == low, g * BCAP + e, pos[0]),
                    jnp.where(held == high, g * BCAP + e, pos[1]),
                )
            return pos

        lo, hi = lax.fori_loop(0, PEERS, find_face, (jnp.int32(0), jnp.int32(0)))
        tab[S_LO + s] = lo
        tab[S_HI + s] = hi

    for c in loads[5:]:
        c.wait()
    finish_rows(0)

    def settle_off(t, _):
        src = tab[S_OFF + t]
        take = src >= 0
        row = jnp.maximum(src, 0)
        half = lax.rem(t, 2)
        base = (t // 4) * 128 + lax.rem(t // 2, 2) * 8
        for c in range(5):
            for a in range(4):
                v = recv_in[row, pl.ds(c * 64 + a * 16, 16), :].astype(F32)
                for b in range(2):
                    rows = pl.ds(pl.multiple_of(base + (2 * a + b) * 16, 8), 8)
                    old = u0o[half, c, rows, :]
                    u0o[half, c, rows, :] = jnp.where(take, v[8 * b : 8 * b + 8], old)
        return 0

    def settle_near(t, _):
        src = tab[S_NEAR + t]
        take = src >= 0
        row = jnp.maximum(src, 0)
        s = t // 8
        base = lax.rem(t, 8) * 8
        for c in range(5):
            for a in range(4):
                v = recv_out[row, pl.ds(c * 64 + a * 16, 16), :].astype(F32)
                for b in range(2):
                    rows = pl.ds(pl.multiple_of(base + (2 * a + b) * 64, 8), 8)
                    old = u0n[s, c, rows, :]
                    u0n[s, c, rows, :] = jnp.where(take, v[8 * b : 8 * b + 8], old)
        return 0


    def halo_copies(st, u):
        return (
            pltpu.make_async_remote_copy(
                u.at[:, :, pl.ds(0, 16), :], xrecv.at[st, 1], hx_send.at[st, 0], hx_recv.at[st, 1],
                device_id=(xdn, gy), device_id_type=MESH,
            ),
            pltpu.make_async_remote_copy(
                u.at[:, :, pl.ds(496, 16), :], xrecv.at[st, 0], hx_send.at[st, 1], hx_recv.at[st, 0],
                device_id=(xup, gy), device_id_type=MESH,
            ),
            pltpu.make_async_remote_copy(
                ysend.at[st, 0], yrecv.at[st, 1], hy_send.at[st, 0], hy_recv.at[st, 1],
                device_id=(gx, ydn), device_id_type=MESH,
            ),
            pltpu.make_async_remote_copy(
                ysend.at[st, 1], yrecv.at[st, 0], hy_send.at[st, 1], hy_recv.at[st, 0],
                device_id=(gx, yup), device_id_type=MESH,
            ),
        )

    def send_halos(st, u):
        for h in range(2):
            for c in range(5):
                for side, first in ((0, 0), (1, 15)):
                    for part in range(2):
                        lo = u[h, c, pl.ds(first + part * 256, 8, stride=16), :]
                        hi = u[h, c, pl.ds(first + part * 256 + 128, 8, stride=16), :]
                        ysend[st, side, h, c, pl.ds(part * 16, 16), :] = jnp.concatenate(
                            [lo, hi], axis=0
                        ).astype(BF16)
        copies = halo_copies(st, u)
        for c in copies:
            c.start()

    def face_copies(st):
        remote = [
            pltpu.make_async_remote_copy(
                fsend.at[st], frecv[st].at[gy], fc_send.at[st, i], fc_recv.at[st, i],
                device_id=(gx, p), device_id_type=MESH,
            )
            for i, p in enumerate(peers)
        ]
        mine = pltpu.make_async_copy(fsend.at[st], frecv[st].at[gy], fc_send.at[st, PEERS - 1])
        return remote, mine

    def send_faces(st, u):
        for s in range(BCAP):
            for c in range(5):
                lo = u[s, c, pl.ds(0, 8, stride=64), :]
                hi = u[s, c, pl.ds(63, 8, stride=64), :]
                fsend[st, s, c] = jnp.concatenate([lo, hi], axis=0).astype(BF16)
        remote, mine = face_copies(st)
        for c in remote:
            c.start()
        mine.start()

    def off_p(u):
        def body(x, _):
            rows = pl.ds(pl.multiple_of(x * 32, 32), 32)
            w = [jnp.concatenate([u[0, c, rows, :], u[1, c, rows, :]], axis=1) for c in range(5)]
            rho, mx, my, mz, en = w
            vx, vy, vz, p, q, h = primitives(w)
            txz, tyz = mx * vz, my * vz
            vals = {
                TXX: mx * vx + p, TXY: mx * vy, TXZ: txz, TYY: my * vy + p, TYZ: tyz,
                HX: h * vx, HY: h * vy, VX: vx, VY: vy, VZ: vz, Q: q, MX: mx, MY: my,
            }
            for k, v in vals.items():
                for e in range(2):
                    so[k, 0, 2 * x + 1 + e, pl.ds(8, 16), :] = v[16 * e : 16 * e + 16, :128]
                    so[k, 1, 2 * x + 1 + e, pl.ds(8, 16), :] = v[16 * e : 16 * e + 16, 128:]
            flux = jnp.concatenate([mz, txz, tyz, mz * vz + p, h * vz], axis=0).astype(BF16)
            visc = jnp.concatenate([vx, vy, vz, q], axis=0) * 1.6
            df = jnp.dot(flux, zoff[0], preferred_element_type=F32)
            sf = jnp.dot(visc.astype(BF16), zoff[1], preferred_element_type=F32)
            for c in range(5):
                r = df[32 * c : 32 * c + 32]
                if c:
                    r = r + sf[32 * c - 32 : 32 * c]
                rzo[0, c, rows, :] = r[:, :128]
                rzo[1, c, rows, :] = r[:, 128:]
            return 0

        lax.fori_loop(0, 16, body, 0, unroll=2)

    def off_ghosts(st):
        for side, plane in ((0, 0), (1, 33)):
            for h in range(2):
                w = [xrecv[st, side, h, c] for c in range(5)]
                for k, v in zip(XK, x_terms(w)):
                    so[k, h, plane, pl.ds(8, 16), :] = v
            for h in range(2):
                w = [yrecv[st, side, h, c].astype(F32) for c in range(5)]
                for i, v in enumerate(y_terms(w)):
                    go[i, side, h] = v

    def off_r(u, a, b):
        first = lax.broadcasted_iota(jnp.int32, (8, 128), 0) == 0
        last = lax.broadcasted_iota(jnp.int32, (8, 128), 0) == 7

        def body(x, _):
            for h in range(2):
                for g in range(2):
                    mid = pl.ds(8 + 8 * g, 8)
                    rows = pl.ds(pl.multiple_of(x * 16 + 8 * g, 8), 8)
                    t = (x // 8) * 4 + g * 2 + h
                    ch = jnp.where(tab[S_OFF + t] >= 0, 0.0, DT * b)
                    yl, yh = [], []
                    for i, k in enumerate(YK):
                        l = so[k, h, x + 1, pl.ds(7 + 8 * g, 8), :]
                        r = so[k, h, x + 1, pl.ds(9 + 8 * g, 8), :]
                        if g == 0:
                            e = jnp.broadcast_to(go[i, 0, h, pl.ds(x, 1), :], (8, 128))
                            l = jnp.where(first, e, l)
                        else:
                            e = jnp.broadcast_to(go[i, 1, h, pl.ds(x, 1), :], (8, 128))
                            r = jnp.where(last, e, r)
                        yl.append(l)
                        yh.append(r)
                    for c in range(5):
                        d = so[XF[c], h, x + 2, mid, :] - so[XF[c], h, x, mid, :]
                        d = d + (yh[c] - yl[c])
                        r = rzo[h, c, rows, :] - 0.5 * d
                        if c:
                            k = VF[c - 1]
                            s = so[k, h, x + 2, mid, :] + so[k, h, x, mid, :]
                            s = s + (yh[4 + c] + yl[4 + c])
                            r = r + (0.8 * s - 3.2 * so[k, h, x + 1, mid, :])
                        v = ch * r + (u[h, c, rows, :] if b == 1.0 else b * u[h, c, rows, :])
                        if a:
                            v = v + a * u0o[h, c, rows, :]
                        uo[h, c, rows, :] = v
            return 0

        lax.fori_loop(0, 32, body, 0, unroll=2)

    def near_p(u):
        def body(i, _):
            s = i // 8
            n = lax.rem(i, 8)
            for ch in range(2):
                rows = pl.ds(pl.multiple_of(n * 64 + ch * 32, 32), 32)
                w = [u[s, c, rows, :] for c in range(5)]
                rho, mx, my, mz, en = w
                vx, vy, vz, p, q, h = primitives(w)
                txz, tyz = mx * vz, my * vz
                vals = {
                    TXX: mx * vx + p, TXY: mx * vy, TXZ: txz, TYY: my * vy + p, TYZ: tyz,
                    HX: h * vx, HY: h * vy, VX: vx, VY: vy, VZ: vz, Q: q, MX: mx, MY: my,
                }
                for k, v in vals.items():
                    sn[k, s, n, pl.ds(8 + ch * 32, 32), :] = v
                flux = jnp.concatenate([mz, txz, tyz, mz * vz + p, h * vz], axis=0).astype(BF16)
                visc = jnp.concatenate([vx, vy, vz, q], axis=0).astype(BF16)
                df = jnp.dot(flux, znear[0], preferred_element_type=F32)
                sf = jnp.dot(visc, znear[1], preferred_element_type=F32)
                gz = met[s, 2, rows, :]
                gz2 = 0.8 * gz * gz
                for c in range(5):
                    r = gz * df[32 * c : 32 * c + 32]
                    if c:
                        r = r + gz2 * sf[32 * c - 32 : 32 * c]
                    rzn[s, c, rows, :] = r
            return 0

        lax.fori_loop(0, 8 * BCAP, body, 0, unroll=2)

    def near_ghosts(st):
        for s in range(BCAP):
            for side, base, part in ((0, S_LO, 8), (1, S_HI, 0)):
                e = tab[base + s]
                w = [
                    frecv[st][lax.div(e, 3), lax.rem(e, 3), c].astype(F32)[part : part + 8]
                    for c in range(5)
                ]
                for i, v in enumerate(y_terms(w)):
                    gn[i, side, s] = v

    def near_r(st, u, a, b, final):
        first = lax.broadcasted_iota(jnp.int32, (8, 128), 0) == 0
        last = lax.broadcasted_iota(jnp.int32, (8, 128), 0) == 7

        def cells(s, n, groups, keep):
            nm = jnp.maximum(n - 1, 0)
            np_ = jnp.minimum(n + 1, 7)
            sign = jnp.where(n == 0, -1.0, 1.0)
            for qd in groups:
                mid = pl.ds(8 + 8 * qd, 8)
                rows = pl.ds(pl.multiple_of(n * 64 + 8 * qd, 8), 8)
                ch = jnp.where(tab[S_NEAR + s * 8 + qd] >= 0, 0.0, DT * b)
                gxm, gym = met[s, 0, rows, :], met[s, 1, rows, :]
                hx, hy = -0.5 * gxm, -0.5 * gym
                gx2, gy2 = 0.8 * gxm * gxm, 0.8 * gym * gym
                yl, yh = [], []
                for i, k in enumerate(YK):
                    l = sn[k, s, n, pl.ds(7 + 8 * qd, 8), :]
                    r = sn[k, s, n, pl.ds(9 + 8 * qd, 8), :]
                    if qd == 0:
                        e = jnp.broadcast_to(gn[i, 0, s, pl.ds(n, 1), :], (8, 128))
                        l = jnp.where(first, e, l)
                    if qd == 7:
                        e = jnp.broadcast_to(gn[i, 1, s, pl.ds(n, 1), :], (8, 128))
                        r = jnp.where(last, e, r)
                    yl.append(l)
                    yh.append(r)
                for c in range(5):
                    lo = sn[XF[c], s, nm, mid, :]
                    if c in (0, 4):
                        lo = sign * lo
                    r = rzn[s, c, rows, :] + hx * (sn[XF[c], s, np_, mid, :] - lo)
                    r = r + hy * (yh[c] - yl[c])
                    if c:
                        k = VF[c - 1]
                        f2 = sn[k, s, n, mid, :]
                        f2 = f2 + f2
                        lo = sn[k, s, nm, mid, :]
                        if c < 4:
                            lo = sign * lo
                        r = r + gx2 * (sn[k, s, np_, mid, :] + lo - f2)
                        r = r + gy2 * (yh[4 + c] + yl[4 + c] - f2)
                    v = ch * r + (u[s, c, rows, :] if b == 1.0 else b * u[s, c, rows, :])
                    if a:
                        v = v + a * u0n[s, c, rows, :]
                    if final:
                        v = jnp.where(keep, v, 0.0)
                    un[s, c, rows, :] = v

        def edges(n, _):
            for s in range(BCAP):
                cells(s, n, (0, 7), tab[S_OCC + s] > 0)
            return 0

        def middle(s):
            keep = tab[S_OCC + s] > 0

            def body(n, _):
                cells(s, n, range(1, 7), keep)
                return 0

            lax.fori_loop(0, 8, body, 0)

        lax.fori_loop(0, 8, edges, 0)
        if not final:
            send_faces(st + 1, un)
        outs = []
        for s in range(BCAP):
            middle(s)
            if final:
                outs.append(pltpu.make_async_copy(un.at[s], near_out.at[s], out_sem.at[2 + s]))
                outs[-1].start()
        return outs

    def off_section(st):
        u = uo if st else u0o
        for c in halo_copies(st, u):
            c.wait_send()
            c.wait_recv()
        off_ghosts(st)
        off_r(u, *RK[st])
        if st < 2:
            send_halos(st + 1, uo)

    def near_section(st):
        remote, mine = face_copies(st)
        mine.wait()
        for c in remote:
            c.wait_send()
            c.wait_recv()
        near_ghosts(st)
        return near_r(st, un if st else u0n, *RK[st], st == 2)

    lax.fori_loop(0, NT_OFF, settle_off, 0)
    send_halos(0, u0o)
    for q in range(4):
        start_rows(1, 4 * q)
    off_p(u0o)
    off_section(0)
    off_p(uo)
    finish_rows(1)
    lax.fori_loop(0, NT_NEAR, settle_near, 0)
    send_faces(0, u0n)
    near_p(u0n)
    off_section(1)
    near_section(0)
    near_p(un)
    off_p(uo)
    near_section(1)
    near_p(un)
    off_section(2)
    oc = [
        pltpu.make_async_copy(uo.at[h], off_out.at[:, :, pl.ds(128 * h, 128)], out_sem.at[h])
        for h in range(2)
    ]
    for c in oc:
        c.start()
    outs = near_section(2)
    for c in oc + outs:
        c.wait()


def advance(fin, fout, slot, faces, off, near, metric, maps_in, maps_out, zoff, znear):
    dma = pltpu.SemaphoreType.DMA
    return pl.pallas_call(
        main_kernel,
        out_shape=(
            jax.ShapeDtypeStruct((5, 512, 256), F32),
            jax.ShapeDtypeStruct((BCAP, 5, 512, 128), F32),
        ),
        in_specs=[pl.BlockSpec(memory_space=pltpu.SMEM)] * 4
        + [pl.BlockSpec(memory_space=pl.ANY)] * 7,
        out_specs=(pl.BlockSpec(memory_space=pl.ANY), pl.BlockSpec(memory_space=pl.ANY)),
        scratch_shapes=[
            pltpu.VMEM((2, 5, 512, 128), F32),
            pltpu.VMEM((BCAP, 5, 512, 128), F32),
            pltpu.VMEM((2, 5, 512, 128), F32),
            pltpu.VMEM((BCAP, 5, 512, 128), F32),
            pltpu.VMEM((BCAP, 3, 512, 128), F32),
            pltpu.VMEM((13, 2, 34, 32, 128), F32),
            pltpu.VMEM((13, BCAP, 8, 80, 128), F32),
            pltpu.VMEM((2, 5, 512, 128), F32),
            pltpu.VMEM((BCAP, 5, 512, 128), F32),
            pltpu.VMEM((NROW, 128, 128), BF16),
            pltpu.VMEM((NROW, 128, 128), BF16),
            pltpu.VMEM((2, 256, 256), BF16),
            pltpu.VMEM((2, 128, 128), BF16),
            pltpu.VMEM((PEERS, 320, 128), BF16),
            pltpu.VMEM((PEERS, 320, 128), BF16),
            pltpu.VMEM((PEERS, 320, 128), BF16),
            pltpu.VMEM((PEERS, 320, 128), BF16),
            pltpu.VMEM((8, 128), jnp.int32),
            pltpu.VMEM((PEERS, 8, 128), jnp.int32),
            pltpu.VMEM((3, BCAP, 5, 16, 128), BF16),
            pltpu.VMEM((PEERS, BCAP, 5, 16, 128), BF16),
            pltpu.VMEM((PEERS, BCAP, 5, 16, 128), BF16),
            pltpu.VMEM((PEERS, BCAP, 5, 16, 128), BF16),
            pltpu.VMEM((3, 2, 2, 5, 16, 128), F32),
            pltpu.VMEM((3, 2, 2, 5, 32, 128), BF16),
            pltpu.VMEM((3, 2, 2, 5, 32, 128), BF16),
            pltpu.VMEM((9, 2, 2, 32, 128), F32),
            pltpu.VMEM((9, 2, BCAP, 8, 128), F32),
            pltpu.SMEM((PEERS, 8, 128), jnp.int32),
            pltpu.SMEM((64,), jnp.int32),
            dma((9,)),
            dma((5,)),
            dma((PEERS,)),
            dma((PEERS,)),
            dma((2, PEERS)),
            dma((2, PEERS)),
            dma((3, PEERS)),
            dma((3, PEERS)),
            dma((3, 2)),
            dma((3, 2)),
            dma((3, 2)),
            dma((3, 2)),
        ],
        compiler_params=pltpu.CompilerParams(
            collective_id=0, has_side_effects=True, vmem_limit_bytes=67043328
        ),
        name="advance",
    )(fin, fout, slot, faces, off, near, metric, maps_in, maps_out, zoff, znear)


def z_matrices(width, wrap):
    col = np.arange(width)
    up, down = np.roll(col, -1), np.roll(col, 1)
    if not wrap:
        up[-1], down[0] = width - 1, 0
    first, second = np.zeros((2, width, width), np.float32)
    scale = 0.5 if wrap else 1.0
    for c in range(width):
        first[up[c], c] -= 0.5
        first[down[c], c] += 0.5
        second[up[c], c] += scale
        second[down[c], c] += scale
        second[c, c] -= 2.0 * scale
    return jnp.asarray(np.stack([first, second]), BF16)


def local(
    off_state,
    near_state,
    near_metric,
    slot_block,
    block_faces,
    fringe_in,
    fringe_in_maps,
    fringe_out,
    fringe_out_maps,
):
    off_next, near_next = advance(
        fringe_in,
        fringe_out,
        slot_block,
        block_faces.T,
        off_state.reshape(5, 512, 256),
        near_state.reshape(BCAP, 5, 512, 128),
        near_metric.reshape(BCAP, 3, 512, 128),
        fringe_in_maps,
        fringe_out_maps,
        z_matrices(256, True),
        z_matrices(128, False),
    )
    return off_next.reshape(off_state.shape), near_next.reshape(near_state.shape)


def solution(mesh):
    in_specs = (
        P(None, "gx", "gy", None),
        P(("gx", "gy"), None, None, None, None),
        P(("gx", "gy"), None, None, None, None),
        P(("gx", "gy")),
        P(),
        P(None, ("gx", "gy")),
        P(("gx", "gy"), None, None),
        P(None, ("gx", "gy")),
        P(("gx", "gy"), None, None),
    )
    out_specs = (P(None, "gx", "gy", None), P(("gx", "gy"), None, None, None, None))
    return jax.shard_map(local, mesh=mesh, in_specs=in_specs, out_specs=out_specs, check_vma=False)
```

```python
import jax
import jax.numpy as jnp
import numpy as np
from jax import lax
from jax.experimental import pallas as pl
from jax.experimental.pallas import tpu as pltpu
from jax.sharding import PartitionSpec as P

MESH = pl.DeviceIdType.MESH
F32 = jnp.float32
BF16 = jnp.bfloat16

TW = 8
TL = 128
BCAP = 3
NROW = 8
NT_OFF = 16
NT_NEAR = 24
PEERS = 16
DT = 0.1
RK = ((0.0, 1.0), (0.75, 0.25), (1.0 / 3.0, 2.0 / 3.0))

TXX, TXY, TXZ, TYY, TYZ, HX, HY, VX, VY, VZ, Q, MX, MY = range(13)
XF = (MX, TXX, TXY, TXZ, HX)
YF = (MY, TXY, TYY, TYZ, HY)
VF = (VX, VY, VZ, Q)
XK = XF + VF
YK = YF + VF

S_OFF, S_NEAR, S_LO, S_HI, S_OCC, S_PICK = 0, 16, 40, 43, 46, 49


def primitives(u):
    rho, mx, my, mz, en = u
    r = 1.0 / rho
    vx, vy, vz = mx * r, my * r, mz * r
    mv = mx * vx + my * vy + mz * vz
    p = 0.4 * en - 0.2 * mv
    q = r * (0.5 * mv + 1.4 * p)
    return vx, vy, vz, p, q, en + p


def x_terms(u):
    vx, vy, vz, p, q, h = primitives(u)
    mx = u[1]
    return (mx, mx * vx + p, mx * vy, mx * vz, h * vx, vx, vy, vz, q)


def y_terms(u):
    vx, vy, vz, p, q, h = primitives(u)
    my = u[2]
    return (my, my * vx, my * vy + p, my * vz, h * vy, vx, vy, vz, q)


OFFSETS = [((2 + i // 4) % 4, (2 + i % 4) % 4) for i in range(16)]
REMOTE = [i for i in range(16) if OFFSETS[i] != (0, 0)]
SELF = OFFSETS.index((0, 0))


def main_kernel(
    fin,
    fout,
    slot,
    faces,
    off,
    near,
    metric,
    maps_in_hbm,
    maps_out_hbm,
    zoff_hbm,
    znear_hbm,
    off_out,
    near_out,
    u0o,
    u0n,
    uo,
    un,
    met,
    so,
    sn,
    rzo,
    rzn,
    maps_in,
    maps_out,
    zoff,
    znear,
    send_in,
    send_out,
    recv_in,
    recv_out,
    tsend,
    trecv,
    fsend,
    frow0,
    frow1,
    frow2,
    psend,
    precv0,
    precv1,
    precv2,
    xrecv,
    ysend,
    yrecv,
    go,
    gn,
    ts,
    tab,
    load_sem,
    out_sem,
    t_send,
    t_recv,
    fr_send,
    fr_recv,
    ra_send,
    ra_recv,
    rb_send,
    rb_recv,
    hx_send,
    hx_recv,
    hy_send,
    hy_recv,
):
    frow = (frow0, frow1, frow2)
    precv = (precv0, precv1, precv2)
    gx = lax.axis_index("gx")
    gy = lax.axis_index("gy")
    nx = 8
    yy, zz = gy // 4, lax.rem(gy, 4)

    def at(dy, dz):
        return lax.rem(yy + dy, 4) * 4 + lax.rem(zz + dz, 4)

    peers = [at(*OFFSETS[i]) for i in REMOTE]
    xup, xdn = lax.rem(gx + 1, nx), lax.rem(gx + nx - 1, nx)
    core = lax.rem(gx, 2)
    ca = core * yy + (1 - core) * zz
    cb = core * zz + (1 - core) * yy

    def on_a(d):
        return at(core * d, (1 - core) * d)

    def on_b(d):
        return at((1 - core) * d, core * d)

    yup, ydn = lax.rem(gy + 1, PEERS), lax.rem(gy + PEERS - 1, PEERS)

    loads = [
        pltpu.make_async_copy(near, u0n, load_sem.at[0]),
        pltpu.make_async_copy(maps_in_hbm, maps_in, load_sem.at[1]),
        pltpu.make_async_copy(off.at[:, :, pl.ds(0, 128)], u0o.at[0], load_sem.at[2]),
        pltpu.make_async_copy(off.at[:, :, pl.ds(128, 128)], u0o.at[1], load_sem.at[3]),
        pltpu.make_async_copy(maps_out_hbm, maps_out, load_sem.at[4]),
        pltpu.make_async_copy(zoff_hbm, zoff, load_sem.at[5]),
        pltpu.make_async_copy(znear_hbm, znear, load_sem.at[6]),
        pltpu.make_async_copy(metric, met, load_sem.at[7]),
    ]
    for c in loads:
        c.start()

    barrier = pltpu.get_barrier_semaphore()
    for p in peers:
        pl.semaphore_signal(barrier, inc=1, device_id=(gx, p), device_id_type=MESH)
    for p in (xup, xdn):
        pl.semaphore_signal(barrier, inc=1, device_id=(p, gy), device_id_type=MESH)

    lane = lax.broadcasted_iota(jnp.int32, (8, 128), 1)
    table = jnp.full((8, 128), -1, jnp.int32)
    for k in range(NROW):
        table = jnp.where(lane == fin[1, k], fin[2, k], table)
        table = jnp.where(lane == 16 + fout[1, k], fout[2, k], table)
    for s in range(BCAP):
        table = jnp.where(lane == 32 + s, slot[s], table)
    tsend[...] = table

    def interpolate(d, first):
        rows_of, maps, out = ((fin, maps_in, send_in), (fout, maps_out, send_out))[d]

        def body(i, _):
            dest = at(2 + i // 4, 2 + lax.rem(i, 4))
            k = jnp.int32(0)
            for r in range(1, NROW):
                k = jnp.where(rows_of[1, r] == dest, r, k)
            t = rows_of[0, k]
            pieces = []
            for c in range(5):
                for n in range(8):
                    if d == 0:
                        at_row = lax.rem(t, 8) * 8 + n * 64
                        pieces.append(u0n[lax.div(t, 8), c, pl.ds(at_row, 8), :])
                    else:
                        at_row = lax.div(t, 4) * 128 + lax.rem(lax.div(t, 2), 2) * 8 + n * 16
                        pieces.append(u0o[lax.rem(t, 2), c, pl.ds(at_row, 8), :])
            x = jnp.concatenate(pieces, axis=0).astype(BF16)
            out[i] = jnp.dot(x, maps[k], preferred_element_type=F32).astype(BF16)
            return 0

        lax.fori_loop(first, first + 4, body, 0)

    def direct(d, i):
        src = (send_in, send_out)[d].at[i]
        dst = (recv_in, recv_out)[d].at[gy]
        if i == SELF:
            return pltpu.make_async_copy(src, dst, fr_send.at[d, i])
        return pltpu.make_async_remote_copy(
            src, dst, fr_send.at[d, i], fr_recv.at[d, i],
            device_id=(gx, at(*OFFSETS[i])), device_id_type=MESH,
        )

    def start_rows(d, first):
        for i in range(first, first + 4):
            direct(d, i).start()

    def finish_rows(d):
        for i in range(16):
            c = direct(d, i)
            if i == SELF:
                c.wait()
            else:
                c.wait_send()
                c.wait_recv()

    loads[0].wait()
    loads[1].wait()
    interpolate(0, 0)
    pl.semaphore_wait(barrier, PEERS + 1)
    tables = [
        pltpu.make_async_remote_copy(
            tsend, trecv.at[gy], t_send.at[i], t_recv.at[i], device_id=(gx, p), device_id_type=MESH
        )
        for i, p in enumerate(peers)
    ]
    own_table = pltpu.make_async_copy(tsend, trecv.at[gy], t_send.at[PEERS - 1])
    for c in tables:
        c.start()
    own_table.start()
    interpolate(0, 4)
    start_rows(0, 0)
    interpolate(0, 8)
    start_rows(0, 4)
    interpolate(0, 12)
    start_rows(0, 8)
    for c in loads[2:5]:
        c.wait()
    interpolate(1, 0)
    start_rows(0, 12)
    interpolate(1, 4)
    interpolate(1, 8)
    interpolate(1, 12)

    own_table.wait()
    for c in tables:
        c.wait_send()
        c.wait_recv()
    to_scalar = pltpu.make_async_copy(trecv, ts, load_sem.at[8])
    to_scalar.start()
    to_scalar.wait()

    def find_off(t, _):
        src = jnp.int32(-1)
        for g in range(PEERS):
            src = jnp.where(ts[g, 0, gy] == t, g, src)
        tab[S_OFF + t] = src
        return 0

    def find_near(t, _):
        src = jnp.int32(-1)
        for g in range(PEERS):
            src = jnp.where(ts[g, 0, 16 + gy] == t, g, src)
        tab[S_NEAR + t] = src
        return 0

    lax.fori_loop(0, NT_OFF, find_off, 0)
    lax.fori_loop(0, NT_NEAR, find_near, 0)
    for s in range(BCAP):
        tab[S_OCC + s] = jnp.where(slot[s] >= 0, 1, 0)
        block = jnp.maximum(slot[s], 0)
        low, high = faces[0, block], faces[1, block]

        def find_face(g, pos):
            for e in range(BCAP):
                held = ts[g, 0, 32 + e]
                pos = (
                    jnp.where(held == low, g * BCAP + e, pos[0]),
                    jnp.where(held == high, g * BCAP + e, pos[1]),
                )
            return pos

        lo, hi = lax.fori_loop(0, PEERS, find_face, (jnp.int32(0), jnp.int32(0)))
        for base, pos in ((S_LO, lo), (S_HI, hi)):
            g = lax.div(pos, BCAP)
            tab[base + s] = jnp.where(core == 0, lax.div(g, 4), lax.rem(g, 4))

    def find_picks(d, _):
        dest = on_b(d)
        for s in range(BCAP):
            block = jnp.maximum(ts[dest, 0, 32 + s], 0)
            low, high = faces[0, block], faces[1, block]
            lo, hi = jnp.int32(0), jnp.int32(0)
            for a in range(4):
                g = core * (a * 4 + zz) + (1 - core) * (yy * 4 + a)
                for e in range(BCAP):
                    held = ts[g, 0, 32 + e]
                    lo = jnp.where(held == low, a * BCAP + e, lo)
                    hi = jnp.where(held == high, a * BCAP + e, hi)
            tab[S_PICK + 6 * d + 2 * s] = lo
            tab[S_PICK + 6 * d + 2 * s + 1] = hi
        return 0

    lax.fori_loop(0, 4, find_picks, 0)

    for c in loads[5:]:
        c.wait()
    finish_rows(0)

    def settle_off(t, _):
        src = tab[S_OFF + t]
        take = src >= 0
        row = jnp.maximum(src, 0)
        half = lax.rem(t, 2)
        base = (t // 4) * 128 + lax.rem(t // 2, 2) * 8
        for c in range(5):
            for a in range(4):
                v = recv_in[row, pl.ds(c * 64 + a * 16, 16), :].astype(F32)
                for b in range(2):
                    rows = pl.ds(pl.multiple_of(base + (2 * a + b) * 16, 8), 8)
                    old = u0o[half, c, rows, :]
                    u0o[half, c, rows, :] = jnp.where(take, v[8 * b : 8 * b + 8], old)
        return 0

    def settle_near(t, _):
        src = tab[S_NEAR + t]
        take = src >= 0
        row = jnp.maximum(src, 0)
        s = t // 8
        base = lax.rem(t, 8) * 8
        for c in range(5):
            for a in range(4):
                v = recv_out[row, pl.ds(c * 64 + a * 16, 16), :].astype(F32)
                for b in range(2):
                    rows = pl.ds(pl.multiple_of(base + (2 * a + b) * 64, 8), 8)
                    old = u0n[s, c, rows, :]
                    u0n[s, c, rows, :] = jnp.where(take, v[8 * b : 8 * b + 8], old)
        return 0


    def halo_copies(st, u):
        return (
            pltpu.make_async_remote_copy(
                u.at[:, :, pl.ds(0, 16), :], xrecv.at[st, 1], hx_send.at[st, 0], hx_recv.at[st, 1],
                device_id=(xdn, gy), device_id_type=MESH,
            ),
            pltpu.make_async_remote_copy(
                u.at[:, :, pl.ds(496, 16), :], xrecv.at[st, 0], hx_send.at[st, 1], hx_recv.at[st, 0],
                device_id=(xup, gy), device_id_type=MESH,
            ),
            pltpu.make_async_remote_copy(
                ysend.at[st, 0], yrecv.at[st, 1], hy_send.at[st, 0], hy_recv.at[st, 1],
                device_id=(gx, ydn), device_id_type=MESH,
            ),
            pltpu.make_async_remote_copy(
                ysend.at[st, 1], yrecv.at[st, 0], hy_send.at[st, 1], hy_recv.at[st, 0],
                device_id=(gx, yup), device_id_type=MESH,
            ),
        )

    def send_halos(st, u):
        for h in range(2):
            for c in range(5):
                for side, first in ((0, 0), (1, 15)):
                    for part in range(2):
                        lo = u[h, c, pl.ds(first + part * 256, 8, stride=16), :]
                        hi = u[h, c, pl.ds(first + part * 256 + 128, 8, stride=16), :]
                        ysend[st, side, h, c, pl.ds(part * 16, 16), :] = jnp.concatenate(
                            [lo, hi], axis=0
                        ).astype(BF16)
        copies = halo_copies(st, u)
        for c in copies:
            c.start()

    def row_copy(st, d):
        return pltpu.make_async_remote_copy(
            fsend.at[st], frow[st].at[ca], ra_send.at[st, d], ra_recv.at[st, d],
            device_id=(gx, on_a(d)), device_id_type=MESH,
        )

    def parcel_copy(st, d):
        return pltpu.make_async_remote_copy(
            psend.at[st, d], precv[st].at[cb], rb_send.at[st, d], rb_recv.at[st, d],
            device_id=(gx, on_b(d)), device_id_type=MESH,
        )

    def send_faces(st, u):
        for s in range(BCAP):
            for c in range(5):
                lo = u[s, c, pl.ds(0, 8, stride=64), :]
                hi = u[s, c, pl.ds(63, 8, stride=64), :]
                both = jnp.concatenate([lo, hi], axis=0).astype(BF16)
                fsend[st, s, c] = both
                frow[st][ca, s, c] = both
        for d in (2, 1, 3):
            row_copy(st, d).start()

    def send_parcels(st):
        for d in (1, 2, 3):
            row_copy(st, d).wait_recv()
        for d in (2, 1, 3, 0):
            for s in range(BCAP):
                lo = tab[S_PICK + 6 * d + 2 * s]
                hi = tab[S_PICK + 6 * d + 2 * s + 1]
                for c in range(5):
                    low = frow[st][lax.div(lo, 3), lax.rem(lo, 3), c].astype(F32)[8:]
                    high = frow[st][lax.div(hi, 3), lax.rem(hi, 3), c].astype(F32)[:8]
                    both = jnp.concatenate([low, high], axis=0).astype(BF16)
                    if d:
                        psend[st, d, s, c] = both
                    else:
                        precv[st][cb, s, c] = both
        for d in (2, 1, 3):
            parcel_copy(st, d).start()

    def finish_faces(st):
        for d in (1, 2, 3):
            row_copy(st, d).wait_send()
            parcel_copy(st, d).wait_send()
            parcel_copy(st, d).wait_recv()

    def off_p(u):
        def body(x, _):
            rows = pl.ds(pl.multiple_of(x * 32, 32), 32)
            w = [jnp.concatenate([u[0, c, rows, :], u[1, c, rows, :]], axis=1) for c in range(5)]
            rho, mx, my, mz, en = w
            vx, vy, vz, p, q, h = primitives(w)
            txz, tyz = mx * vz, my * vz
            vals = {
                TXX: mx * vx + p, TXY: mx * vy, TXZ: txz, TYY: my * vy + p, TYZ: tyz,
                HX: h * vx, HY: h * vy, VX: vx, VY: vy, VZ: vz, Q: q, MX: mx, MY: my,
            }
            for k, v in vals.items():
                for e in range(2):
                    so[k, 0, 2 * x + 1 + e, pl.ds(8, 16), :] = v[16 * e : 16 * e + 16, :128]
                    so[k, 1, 2 * x + 1 + e, pl.ds(8, 16), :] = v[16 * e : 16 * e + 16, 128:]
            flux = jnp.concatenate([mz, txz, tyz, mz * vz + p, h * vz], axis=0).astype(BF16)
            visc = jnp.concatenate([vx, vy, vz, q], axis=0) * 1.6
            df = jnp.dot(flux, zoff[0], preferred_element_type=F32)
            sf = jnp.dot(visc.astype(BF16), zoff[1], preferred_element_type=F32)
            for c in range(5):
                r = df[32 * c : 32 * c + 32]
                if c:
                    r = r + sf[32 * c - 32 : 32 * c]
                rzo[0, c, rows, :] = r[:, :128]
                rzo[1, c, rows, :] = r[:, 128:]
            return 0

        lax.fori_loop(0, 16, body, 0, unroll=2)

    def off_ghosts(st):
        for side, plane in ((0, 0), (1, 33)):
            for h in range(2):
                w = [xrecv[st, side, h, c] for c in range(5)]
                for k, v in zip(XK, x_terms(w)):
                    so[k, h, plane, pl.ds(8, 16), :] = v
            for h in range(2):
                w = [yrecv[st, side, h, c].astype(F32) for c in range(5)]
                for i, v in enumerate(y_terms(w)):
                    go[i, side, h] = v

    def off_r(u, a, b):
        first = lax.broadcasted_iota(jnp.int32, (8, 128), 0) == 0
        last = lax.broadcasted_iota(jnp.int32, (8, 128), 0) == 7

        def body(x, _):
            for h in range(2):
                for g in range(2):
                    mid = pl.ds(8 + 8 * g, 8)
                    rows = pl.ds(pl.multiple_of(x * 16 + 8 * g, 8), 8)
                    t = (x // 8) * 4 + g * 2 + h
                    ch = jnp.where(tab[S_OFF + t] >= 0, 0.0, DT * b)
                    yl, yh = [], []
                    for i, k in enumerate(YK):
                        l = so[k, h, x + 1, pl.ds(7 + 8 * g, 8), :]
                        r = so[k, h, x + 1, pl.ds(9 + 8 * g, 8), :]
                        if g == 0:
                            e = jnp.broadcast_to(go[i, 0, h, pl.ds(x, 1), :], (8, 128))
                            l = jnp.where(first, e, l)
                        else:
                            e = jnp.broadcast_to(go[i, 1, h, pl.ds(x, 1), :], (8, 128))
                            r = jnp.where(last, e, r)
                        yl.append(l)
                        yh.append(r)
                    for c in range(5):
                        d = so[XF[c], h, x + 2, mid, :] - so[XF[c], h, x, mid, :]
                        d = d + (yh[c] - yl[c])
                        r = rzo[h, c, rows, :] - 0.5 * d
                        if c:
                            k = VF[c - 1]
                            s = so[k, h, x + 2, mid, :] + so[k, h, x, mid, :]
                            s = s + (yh[4 + c] + yl[4 + c])
                            r = r + (0.8 * s - 3.2 * so[k, h, x + 1, mid, :])
                        v = ch * r + (u[h, c, rows, :] if b == 1.0 else b * u[h, c, rows, :])
                        if a:
                            v = v + a * u0o[h, c, rows, :]
                        uo[h, c, rows, :] = v
            return 0

        lax.fori_loop(0, 32, body, 0, unroll=2)

    def near_p(u):
        def body(i, _):
            s = i // 8
            n = lax.rem(i, 8)
            for ch in range(2):
                rows = pl.ds(pl.multiple_of(n * 64 + ch * 32, 32), 32)
                w = [u[s, c, rows, :] for c in range(5)]
                rho, mx, my, mz, en = w
                vx, vy, vz, p, q, h = primitives(w)
                txz, tyz = mx * vz, my * vz
                vals = {
                    TXX: mx * vx + p, TXY: mx * vy, TXZ: txz, TYY: my * vy + p, TYZ: tyz,
                    HX: h * vx, HY: h * vy, VX: vx, VY: vy, VZ: vz, Q: q, MX: mx, MY: my,
                }
                for k, v in vals.items():
                    sn[k, s, n, pl.ds(8 + ch * 32, 32), :] = v
                flux = jnp.concatenate([mz, txz, tyz, mz * vz + p, h * vz], axis=0).astype(BF16)
                visc = jnp.concatenate([vx, vy, vz, q], axis=0).astype(BF16)
                df = jnp.dot(flux, znear[0], preferred_element_type=F32)
                sf = jnp.dot(visc, znear[1], preferred_element_type=F32)
                gz = met[s, 2, rows, :]
                gz2 = 0.8 * gz * gz
                for c in range(5):
                    r = gz * df[32 * c : 32 * c + 32]
                    if c:
                        r = r + gz2 * sf[32 * c - 32 : 32 * c]
                    rzn[s, c, rows, :] = r
            return 0

        lax.fori_loop(0, 8 * BCAP, body, 0, unroll=2)

    def near_ghosts(st):
        for s in range(BCAP):
            for side, base in ((0, S_LO), (1, S_HI)):
                row = tab[base + s]
                w = [
                    precv[st][row, s, c].astype(F32)[8 * side : 8 * side + 8] for c in range(5)
                ]
                for i, v in enumerate(y_terms(w)):
                    gn[i, side, s] = v

    def near_r(st, u, a, b, final):
        first = lax.broadcasted_iota(jnp.int32, (8, 128), 0) == 0
        last = lax.broadcasted_iota(jnp.int32, (8, 128), 0) == 7

        def cells(s, n, groups, keep):
            nm = jnp.maximum(n - 1, 0)
            np_ = jnp.minimum(n + 1, 7)
            sign = jnp.where(n == 0, -1.0, 1.0)
            for qd in groups:
                mid = pl.ds(8 + 8 * qd, 8)
                rows = pl.ds(pl.multiple_of(n * 64 + 8 * qd, 8), 8)
                ch = jnp.where(tab[S_NEAR + s * 8 + qd] >= 0, 0.0, DT * b)
                gxm, gym = met[s, 0, rows, :], met[s, 1, rows, :]
                hx, hy = -0.5 * gxm, -0.5 * gym
                gx2, gy2 = 0.8 * gxm * gxm, 0.8 * gym * gym
                yl, yh = [], []
                for i, k in enumerate(YK):
                    l = sn[k, s, n, pl.ds(7 + 8 * qd, 8), :]
                    r = sn[k, s, n, pl.ds(9 + 8 * qd, 8), :]
                    if qd == 0:
                        e = jnp.broadcast_to(gn[i, 0, s, pl.ds(n, 1), :], (8, 128))
                        l = jnp.where(first, e, l)
                    if qd == 7:
                        e = jnp.broadcast_to(gn[i, 1, s, pl.ds(n, 1), :], (8, 128))
                        r = jnp.where(last, e, r)
                    yl.append(l)
                    yh.append(r)
                for c in range(5):
                    lo = sn[XF[c], s, nm, mid, :]
                    if c in (0, 4):
                        lo = sign * lo
                    r = rzn[s, c, rows, :] + hx * (sn[XF[c], s, np_, mid, :] - lo)
                    r = r + hy * (yh[c] - yl[c])
                    if c:
                        k = VF[c - 1]
                        f2 = sn[k, s, n, mid, :]
                        f2 = f2 + f2
                        lo = sn[k, s, nm, mid, :]
                        if c < 4:
                            lo = sign * lo
                        r = r + gx2 * (sn[k, s, np_, mid, :] + lo - f2)
                        r = r + gy2 * (yh[4 + c] + yl[4 + c] - f2)
                    v = ch * r + (u[s, c, rows, :] if b == 1.0 else b * u[s, c, rows, :])
                    if a:
                        v = v + a * u0n[s, c, rows, :]
                    if final:
                        v = jnp.where(keep, v, 0.0)
                    un[s, c, rows, :] = v

        def edges(n, _):
            for s in range(BCAP):
                cells(s, n, (0, 7), tab[S_OCC + s] > 0)
            return 0

        def middle(s):
            keep = tab[S_OCC + s] > 0

            def body(n, _):
                cells(s, n, range(1, 7), keep)
                return 0

            lax.fori_loop(0, 8, body, 0)

        lax.fori_loop(0, 8, edges, 0)
        if not final:
            send_faces(st + 1, un)
        outs = []
        for s in range(BCAP):
            middle(s)
            if s == 1 and not final:
                send_parcels(st + 1)
            if final:
                outs.append(pltpu.make_async_copy(un.at[s], near_out.at[s], out_sem.at[2 + s]))
                outs[-1].start()
        return outs

    def off_section(st):
        u = uo if st else u0o
        for c in halo_copies(st, u):
            c.wait_send()
            c.wait_recv()
        off_ghosts(st)
        off_r(u, *RK[st])
        if st < 2:
            send_halos(st + 1, uo)

    def near_section(st):
        finish_faces(st)
        near_ghosts(st)
        return near_r(st, un if st else u0n, *RK[st], st == 2)

    lax.fori_loop(0, NT_OFF, settle_off, 0)
    send_halos(0, u0o)
    start_rows(1, 0)
    start_rows(1, 4)
    off_p(u0o)
    off_section(0)
    start_rows(1, 8)
    start_rows(1, 12)
    off_p(uo)
    off_section(1)
    off_p(uo)
    finish_rows(1)
    lax.fori_loop(0, NT_NEAR, settle_near, 0)
    send_faces(0, u0n)
    near_p(u0n)
    send_parcels(0)
    off_section(2)
    oc = [
        pltpu.make_async_copy(uo.at[h], off_out.at[:, :, pl.ds(128 * h, 128)], out_sem.at[h])
        for h in range(2)
    ]
    for c in oc:
        c.start()
    near_section(0)
    near_p(un)
    near_section(1)
    near_p(un)
    outs = near_section(2)
    for c in oc + outs:
        c.wait()


def advance(fin, fout, slot, faces, off, near, metric, maps_in, maps_out, zoff, znear):
    dma = pltpu.SemaphoreType.DMA
    return pl.pallas_call(
        main_kernel,
        out_shape=(
            jax.ShapeDtypeStruct((5, 512, 256), F32),
            jax.ShapeDtypeStruct((BCAP, 5, 512, 128), F32),
        ),
        in_specs=[pl.BlockSpec(memory_space=pltpu.SMEM)] * 4
        + [pl.BlockSpec(memory_space=pl.ANY)] * 7,
        out_specs=(pl.BlockSpec(memory_space=pl.ANY), pl.BlockSpec(memory_space=pl.ANY)),
        scratch_shapes=[
            pltpu.VMEM((2, 5, 512, 128), F32),
            pltpu.VMEM((BCAP, 5, 512, 128), F32),
            pltpu.VMEM((2, 5, 512, 128), F32),
            pltpu.VMEM((BCAP, 5, 512, 128), F32),
            pltpu.VMEM((BCAP, 3, 512, 128), F32),
            pltpu.VMEM((13, 2, 34, 32, 128), F32),
            pltpu.VMEM((13, BCAP, 8, 80, 128), F32),
            pltpu.VMEM((2, 5, 512, 128), F32),
            pltpu.VMEM((BCAP, 5, 512, 128), F32),
            pltpu.VMEM((NROW, 128, 128), BF16),
            pltpu.VMEM((NROW, 128, 128), BF16),
            pltpu.VMEM((2, 256, 256), BF16),
            pltpu.VMEM((2, 128, 128), BF16),
            pltpu.VMEM((PEERS, 320, 128), BF16),
            pltpu.VMEM((PEERS, 320, 128), BF16),
            pltpu.VMEM((PEERS, 320, 128), BF16),
            pltpu.VMEM((PEERS, 320, 128), BF16),
            pltpu.VMEM((8, 128), jnp.int32),
            pltpu.VMEM((PEERS, 8, 128), jnp.int32),
            pltpu.VMEM((3, BCAP, 5, 16, 128), BF16),
            pltpu.VMEM((4, BCAP, 5, 16, 128), BF16),
            pltpu.VMEM((4, BCAP, 5, 16, 128), BF16),
            pltpu.VMEM((4, BCAP, 5, 16, 128), BF16),
            pltpu.VMEM((3, 4, BCAP, 5, 16, 128), BF16),
            pltpu.VMEM((4, BCAP, 5, 16, 128), BF16),
            pltpu.VMEM((4, BCAP, 5, 16, 128), BF16),
            pltpu.VMEM((4, BCAP, 5, 16, 128), BF16),
            pltpu.VMEM((3, 2, 2, 5, 16, 128), F32),
            pltpu.VMEM((3, 2, 2, 5, 32, 128), BF16),
            pltpu.VMEM((3, 2, 2, 5, 32, 128), BF16),
            pltpu.VMEM((9, 2, 2, 32, 128), F32),
            pltpu.VMEM((9, 2, BCAP, 8, 128), F32),
            pltpu.SMEM((PEERS, 8, 128), jnp.int32),
            pltpu.SMEM((80,), jnp.int32),
            dma((9,)),
            dma((5,)),
            dma((PEERS,)),
            dma((PEERS,)),
            dma((2, PEERS)),
            dma((2, PEERS)),
            dma((3, 4)),
            dma((3, 4)),
            dma((3, 4)),
            dma((3, 4)),
            dma((3, 2)),
            dma((3, 2)),
            dma((3, 2)),
            dma((3, 2)),
        ],
        compiler_params=pltpu.CompilerParams(
            collective_id=0, has_side_effects=True, vmem_limit_bytes=67043328
        ),
        name="advance",
    )(fin, fout, slot, faces, off, near, metric, maps_in, maps_out, zoff, znear)


def z_matrices(width, wrap):
    col = np.arange(width)
    up, down = np.roll(col, -1), np.roll(col, 1)
    if not wrap:
        up[-1], down[0] = width - 1, 0
    first, second = np.zeros((2, width, width), np.float32)
    scale = 0.5 if wrap else 1.0
    for c in range(width):
        first[up[c], c] -= 0.5
        first[down[c], c] += 0.5
        second[up[c], c] += scale
        second[down[c], c] += scale
        second[c, c] -= 2.0 * scale
    return jnp.asarray(np.stack([first, second]), BF16)


def local(
    off_state,
    near_state,
    near_metric,
    slot_block,
    block_faces,
    fringe_in,
    fringe_in_maps,
    fringe_out,
    fringe_out_maps,
):
    off_next, near_next = advance(
        fringe_in,
        fringe_out,
        slot_block,
        block_faces.T,
        off_state.reshape(5, 512, 256),
        near_state.reshape(BCAP, 5, 512, 128),
        near_metric.reshape(BCAP, 3, 512, 128),
        fringe_in_maps,
        fringe_out_maps,
        z_matrices(256, True),
        z_matrices(128, False),
    )
    return off_next.reshape(off_state.shape), near_next.reshape(near_state.shape)


def solution(mesh):
    in_specs = (
        P(None, "gx", "gy", None),
        P(("gx", "gy"), None, None, None, None),
        P(("gx", "gy"), None, None, None, None),
        P(("gx", "gy")),
        P(),
        P(None, ("gx", "gy")),
        P(("gx", "gy"), None, None),
        P(None, ("gx", "gy")),
        P(("gx", "gy"), None, None),
    )
    out_specs = (P(None, "gx", "gy", None), P(("gx", "gy"), None, None, None, None))
    return jax.shard_map(local, mesh=mesh, in_specs=in_specs, out_specs=out_specs, check_vma=False)
```

```python
import jax
import jax.numpy as jnp
import numpy as np
from jax import lax
from jax.experimental import pallas as pl
from jax.experimental.pallas import tpu as pltpu
from jax.sharding import PartitionSpec as P

MESH = pl.DeviceIdType.MESH
F32 = jnp.float32
BF16 = jnp.bfloat16

TW = 8
TL = 128
BCAP = 3
NROW = 8
NT_OFF = 16
NT_NEAR = 24
PEERS = 16
DT = 0.1
RK = ((0.0, 1.0), (0.75, 0.25), (1.0 / 3.0, 2.0 / 3.0))

TXX, TXY, TXZ, TYY, TYZ, HX, HY, VX, VY, VZ, Q, MX, MY = range(13)
XF = (MX, TXX, TXY, TXZ, HX)
YF = (MY, TXY, TYY, TYZ, HY)
VF = (VX, VY, VZ, Q)
XK = XF + VF
YK = YF + VF

S_OFF, S_NEAR, S_LO, S_HI, S_OCC, S_PICK = 0, 16, 40, 43, 46, 49


def primitives(u):
    rho, mx, my, mz, en = u
    r = 1.0 / rho
    vx, vy, vz = mx * r, my * r, mz * r
    mv = mx * vx + my * vy + mz * vz
    p = 0.4 * en - 0.2 * mv
    q = r * (0.5 * mv + 1.4 * p)
    return vx, vy, vz, p, q, en + p


def x_terms(u):
    vx, vy, vz, p, q, h = primitives(u)
    mx = u[1]
    return (mx, mx * vx + p, mx * vy, mx * vz, h * vx, vx, vy, vz, q)


def y_terms(u):
    vx, vy, vz, p, q, h = primitives(u)
    my = u[2]
    return (my, my * vx, my * vy + p, my * vz, h * vy, vx, vy, vz, q)


OFFSETS = [((2 + i // 4) % 4, (2 + i % 4) % 4) for i in range(16)]
REMOTE = [i for i in range(16) if OFFSETS[i] != (0, 0)]
SELF = OFFSETS.index((0, 0))


def main_kernel(
    fin,
    fout,
    slot,
    faces,
    off,
    near,
    metric,
    maps_in_hbm,
    maps_out_hbm,
    zoff_hbm,
    znear_hbm,
    off_out,
    near_out,
    u0o,
    u0n,
    uo,
    un,
    met,
    so,
    sn,
    rzo,
    rzn,
    maps_in,
    maps_out,
    zoff,
    znear,
    send_in,
    send_out,
    recv_in,
    recv_out,
    tsend,
    trecv,
    fsend,
    frow0,
    frow1,
    frow2,
    psend,
    precv0,
    precv1,
    precv2,
    xrecv,
    ysend,
    yrecv,
    go,
    gn,
    ts,
    tab,
    load_sem,
    out_sem,
    t_send,
    t_recv,
    fr_send,
    fr_recv,
    ra_send,
    ra_recv,
    rb_send,
    rb_recv,
    hx_send,
    hx_recv,
    hy_send,
    hy_recv,
):
    frow = (frow0, frow1, frow2)
    precv = (precv0, precv1, precv2)
    gx = lax.axis_index("gx")
    gy = lax.axis_index("gy")
    nx = 8
    yy, zz = gy // 4, lax.rem(gy, 4)

    def at(dy, dz):
        return lax.rem(yy + dy, 4) * 4 + lax.rem(zz + dz, 4)

    peers = [at(*OFFSETS[i]) for i in REMOTE]
    xup, xdn = lax.rem(gx + 1, nx), lax.rem(gx + nx - 1, nx)
    core = lax.rem(gx, 2)
    ca = core * yy + (1 - core) * zz
    cb = core * zz + (1 - core) * yy

    def on_a(d):
        return at(core * d, (1 - core) * d)

    def on_b(d):
        return at((1 - core) * d, core * d)

    yup, ydn = lax.rem(gy + 1, PEERS), lax.rem(gy + PEERS - 1, PEERS)

    loads = [
        pltpu.make_async_copy(near, u0n, load_sem.at[0]),
        pltpu.make_async_copy(maps_in_hbm, maps_in, load_sem.at[1]),
        pltpu.make_async_copy(off.at[:, :, pl.ds(0, 128)], u0o.at[0], load_sem.at[2]),
        pltpu.make_async_copy(off.at[:, :, pl.ds(128, 128)], u0o.at[1], load_sem.at[3]),
        pltpu.make_async_copy(maps_out_hbm, maps_out, load_sem.at[4]),
        pltpu.make_async_copy(zoff_hbm, zoff, load_sem.at[5]),
        pltpu.make_async_copy(znear_hbm, znear, load_sem.at[6]),
        pltpu.make_async_copy(metric, met, load_sem.at[7]),
    ]
    for c in loads:
        c.start()

    barrier = pltpu.get_barrier_semaphore()
    for p in peers:
        pl.semaphore_signal(barrier, inc=1, device_id=(gx, p), device_id_type=MESH)
    for p in (xup, xdn):
        pl.semaphore_signal(barrier, inc=1, device_id=(p, gy), device_id_type=MESH)

    lane = lax.broadcasted_iota(jnp.int32, (8, 128), 1)
    table = jnp.full((8, 128), -1, jnp.int32)
    for k in range(NROW):
        table = jnp.where(lane == fin[1, k], fin[2, k], table)
        table = jnp.where(lane == 16 + fout[1, k], fout[2, k], table)
    for s in range(BCAP):
        table = jnp.where(lane == 32 + s, slot[s], table)
    tsend[...] = table

    def interpolate(d, first):
        rows_of, maps, out = ((fin, maps_in, send_in), (fout, maps_out, send_out))[d]

        def body(i, _):
            dest = at(2 + i // 4, 2 + lax.rem(i, 4))
            k = jnp.int32(0)
            for r in range(1, NROW):
                k = jnp.where(rows_of[1, r] == dest, r, k)
            t = rows_of[0, k]
            pieces = []
            for c in range(5):
                for n in range(8):
                    if d == 0:
                        at_row = lax.rem(t, 8) * 8 + n * 64
                        pieces.append(u0n[lax.div(t, 8), c, pl.ds(at_row, 8), :])
                    else:
                        at_row = lax.div(t, 4) * 128 + lax.rem(lax.div(t, 2), 2) * 8 + n * 16
                        pieces.append(u0o[lax.rem(t, 2), c, pl.ds(at_row, 8), :])
            x = jnp.concatenate(pieces, axis=0).astype(BF16)
            out[i] = jnp.dot(x, maps[k], preferred_element_type=F32).astype(BF16)
            return 0

        lax.fori_loop(first, first + 4, body, 0)

    def direct(d, i):
        src = (send_in, send_out)[d].at[i]
        dst = (recv_in, recv_out)[d].at[gy]
        if i == SELF:
            return pltpu.make_async_copy(src, dst, fr_send.at[d, i])
        return pltpu.make_async_remote_copy(
            src, dst, fr_send.at[d, i], fr_recv.at[d, i],
            device_id=(gx, at(*OFFSETS[i])), device_id_type=MESH,
        )

    def start_rows(d, first):
        for i in range(first, first + 4):
            direct(d, i).start()

    def finish_rows(d):
        for i in range(16):
            c = direct(d, i)
            if i == SELF:
                c.wait()
            else:
                c.wait_send()
                c.wait_recv()

    loads[0].wait()
    loads[1].wait()
    interpolate(0, 0)
    pl.semaphore_wait(barrier, PEERS + 1)
    tables = [
        pltpu.make_async_remote_copy(
            tsend, trecv.at[gy], t_send.at[i], t_recv.at[i], device_id=(gx, p), device_id_type=MESH
        )
        for i, p in enumerate(peers)
    ]
    own_table = pltpu.make_async_copy(tsend, trecv.at[gy], t_send.at[PEERS - 1])
    for c in tables:
        c.start()
    own_table.start()
    interpolate(0, 4)
    start_rows(0, 0)
    interpolate(0, 8)
    start_rows(0, 4)
    interpolate(0, 12)
    start_rows(0, 8)
    for c in loads[2:5]:
        c.wait()
    interpolate(1, 0)
    start_rows(0, 12)
    interpolate(1, 4)
    interpolate(1, 8)
    interpolate(1, 12)

    own_table.wait()
    for c in tables:
        c.wait_send()
        c.wait_recv()
    to_scalar = pltpu.make_async_copy(trecv, ts, load_sem.at[8])
    to_scalar.start()
    to_scalar.wait()

    def find_off(t, _):
        src = jnp.int32(-1)
        for g in range(PEERS):
            src = jnp.where(ts[g, 0, gy] == t, g, src)
        tab[S_OFF + t] = src
        return 0

    def find_near(t, _):
        src = jnp.int32(-1)
        for g in range(PEERS):
            src = jnp.where(ts[g, 0, 16 + gy] == t, g, src)
        tab[S_NEAR + t] = src
        return 0

    lax.fori_loop(0, NT_OFF, find_off, 0)
    lax.fori_loop(0, NT_NEAR, find_near, 0)
    for s in range(BCAP):
        tab[S_OCC + s] = jnp.where(slot[s] >= 0, 1, 0)
        block = jnp.maximum(slot[s], 0)
        low, high = faces[0, block], faces[1, block]

        def find_face(g, pos):
            for e in range(BCAP):
                held = ts[g, 0, 32 + e]
                pos = (
                    jnp.where(held == low, g * BCAP + e, pos[0]),
                    jnp.where(held == high, g * BCAP + e, pos[1]),
                )
            return pos

        lo, hi = lax.fori_loop(0, PEERS, find_face, (jnp.int32(0), jnp.int32(0)))
        for base, pos in ((S_LO, lo), (S_HI, hi)):
            g = lax.div(pos, BCAP)
            tab[base + s] = jnp.where(core == 0, lax.div(g, 4), lax.rem(g, 4))

    def find_picks(d, _):
        dest = on_b(d)
        for s in range(BCAP):
            block = jnp.maximum(ts[dest, 0, 32 + s], 0)
            low, high = faces[0, block], faces[1, block]
            lo, hi = jnp.int32(0), jnp.int32(0)
            for a in range(4):
                g = core * (a * 4 + zz) + (1 - core) * (yy * 4 + a)
                for e in range(BCAP):
                    held = ts[g, 0, 32 + e]
                    lo = jnp.where(held == low, a * BCAP + e, lo)
                    hi = jnp.where(held == high, a * BCAP + e, hi)
            tab[S_PICK + 6 * d + 2 * s] = lo
            tab[S_PICK + 6 * d + 2 * s + 1] = hi
        return 0

    lax.fori_loop(0, 4, find_picks, 0)

    for c in loads[5:]:
        c.wait()
    finish_rows(0)

    def settle_off(t, _):
        src = tab[S_OFF + t]
        take = src >= 0
        row = jnp.maximum(src, 0)
        half = lax.rem(t, 2)
        base = (t // 4) * 128 + lax.rem(t // 2, 2) * 8
        for c in range(5):
            for a in range(4):
                v = recv_in[row, pl.ds(c * 64 + a * 16, 16), :].astype(F32)
                for b in range(2):
                    rows = pl.ds(pl.multiple_of(base + (2 * a + b) * 16, 8), 8)
                    old = u0o[half, c, rows, :]
                    u0o[half, c, rows, :] = jnp.where(take, v[8 * b : 8 * b + 8], old)
        return 0

    def settle_near(t, _):
        src = tab[S_NEAR + t]
        take = src >= 0
        row = jnp.maximum(src, 0)
        s = t // 8
        base = lax.rem(t, 8) * 8
        for c in range(5):
            for a in range(4):
                v = recv_out[row, pl.ds(c * 64 + a * 16, 16), :].astype(F32)
                for b in range(2):
                    rows = pl.ds(pl.multiple_of(base + (2 * a + b) * 64, 8), 8)
                    old = u0n[s, c, rows, :]
                    u0n[s, c, rows, :] = jnp.where(take, v[8 * b : 8 * b + 8], old)
        return 0


    def halo_copies(st, u):
        return (
            pltpu.make_async_remote_copy(
                u.at[:, :, pl.ds(0, 16), :], xrecv.at[st, 1], hx_send.at[st, 0], hx_recv.at[st, 1],
                device_id=(xdn, gy), device_id_type=MESH,
            ),
            pltpu.make_async_remote_copy(
                u.at[:, :, pl.ds(496, 16), :], xrecv.at[st, 0], hx_send.at[st, 1], hx_recv.at[st, 0],
                device_id=(xup, gy), device_id_type=MESH,
            ),
            pltpu.make_async_remote_copy(
                ysend.at[st, 0], yrecv.at[st, 1], hy_send.at[st, 0], hy_recv.at[st, 1],
                device_id=(gx, ydn), device_id_type=MESH,
            ),
            pltpu.make_async_remote_copy(
                ysend.at[st, 1], yrecv.at[st, 0], hy_send.at[st, 1], hy_recv.at[st, 0],
                device_id=(gx, yup), device_id_type=MESH,
            ),
        )

    def send_halos(st, u):
        for h in range(2):
            for c in range(5):
                for side, first in ((0, 0), (1, 15)):
                    for part in range(2):
                        lo = u[h, c, pl.ds(first + part * 256, 8, stride=16), :]
                        hi = u[h, c, pl.ds(first + part * 256 + 128, 8, stride=16), :]
                        ysend[st, side, h, c, pl.ds(part * 16, 16), :] = jnp.concatenate(
                            [lo, hi], axis=0
                        ).astype(BF16)
        copies = halo_copies(st, u)
        for c in copies:
            c.start()

    def row_copy(st, d):
        return pltpu.make_async_remote_copy(
            fsend.at[st], frow[st].at[ca], ra_send.at[st, d], ra_recv.at[st, d],
            device_id=(gx, on_a(d)), device_id_type=MESH,
        )

    def parcel_copy(st, d):
        return pltpu.make_async_remote_copy(
            psend.at[st, d], precv[st].at[cb], rb_send.at[st, d], rb_recv.at[st, d],
            device_id=(gx, on_b(d)), device_id_type=MESH,
        )

    def send_faces(st, u):
        for s in range(BCAP):
            for c in range(5):
                lo = u[s, c, pl.ds(0, 8, stride=64), :]
                hi = u[s, c, pl.ds(63, 8, stride=64), :]
                both = jnp.concatenate([lo, hi], axis=0).astype(BF16)
                fsend[st, s, c] = both
                frow[st][ca, s, c] = both
        for d in (2, 1, 3):
            row_copy(st, d).start()

    def send_parcels(st):
        for d in (1, 2, 3):
            row_copy(st, d).wait_recv()
        for d in (2, 1, 3, 0):
            for s in range(BCAP):
                lo = tab[S_PICK + 6 * d + 2 * s]
                hi = tab[S_PICK + 6 * d + 2 * s + 1]
                for c in range(5):
                    low = frow[st][lax.div(lo, 3), lax.rem(lo, 3), c].astype(F32)[8:]
                    high = frow[st][lax.div(hi, 3), lax.rem(hi, 3), c].astype(F32)[:8]
                    both = jnp.concatenate([low, high], axis=0).astype(BF16)
                    if d:
                        psend[st, d, s, c] = both
                    else:
                        precv[st][cb, s, c] = both
        for d in (2, 1, 3):
            parcel_copy(st, d).start()

    def finish_faces(st):
        for d in (1, 2, 3):
            row_copy(st, d).wait_send()
            parcel_copy(st, d).wait_send()
            parcel_copy(st, d).wait_recv()

    def off_p(u):
        def body(x, _):
            rows = pl.ds(pl.multiple_of(x * 32, 32), 32)
            w = [jnp.concatenate([u[0, c, rows, :], u[1, c, rows, :]], axis=1) for c in range(5)]
            rho, mx, my, mz, en = w
            vx, vy, vz, p, q, h = primitives(w)
            txz, tyz = mx * vz, my * vz
            vals = {
                TXX: mx * vx + p, TXY: mx * vy, TXZ: txz, TYY: my * vy + p, TYZ: tyz,
                HX: h * vx, HY: h * vy, VX: vx, VY: vy, VZ: vz, Q: q, MX: mx, MY: my,
            }
            for k, v in vals.items():
                for e in range(2):
                    so[k, 0, 2 * x + 1 + e, pl.ds(8, 16), :] = v[16 * e : 16 * e + 16, :128]
                    so[k, 1, 2 * x + 1 + e, pl.ds(8, 16), :] = v[16 * e : 16 * e + 16, 128:]
            flux = jnp.concatenate([mz, txz, tyz, mz * vz + p, h * vz], axis=0).astype(BF16)
            visc = jnp.concatenate([vx, vy, vz, q], axis=0) * 1.6
            df = jnp.dot(flux, zoff[0], preferred_element_type=F32)
            sf = jnp.dot(visc.astype(BF16), zoff[1], preferred_element_type=F32)
            for c in range(5):
                r = df[32 * c : 32 * c + 32]
                if c:
                    r = r + sf[32 * c - 32 : 32 * c]
                rzo[0, c, rows, :] = r[:, :128]
                rzo[1, c, rows, :] = r[:, 128:]
            return 0

        lax.fori_loop(0, 16, body, 0, unroll=2)

    def off_ghosts(st):
        for side, plane in ((0, 0), (1, 33)):
            for h in range(2):
                w = [xrecv[st, side, h, c] for c in range(5)]
                for k, v in zip(XK, x_terms(w)):
                    so[k, h, plane, pl.ds(8, 16), :] = v
            for h in range(2):
                w = [yrecv[st, side, h, c].astype(F32) for c in range(5)]
                for i, v in enumerate(y_terms(w)):
                    go[i, side, h] = v

    def off_r(u, a, b):
        first = lax.broadcasted_iota(jnp.int32, (8, 128), 0) == 0
        last = lax.broadcasted_iota(jnp.int32, (8, 128), 0) == 7

        def body(x, _):
            for h in range(2):
                for g in range(2):
                    mid = pl.ds(8 + 8 * g, 8)
                    rows = pl.ds(pl.multiple_of(x * 16 + 8 * g, 8), 8)
                    t = (x // 8) * 4 + g * 2 + h
                    ch = jnp.where(tab[S_OFF + t] >= 0, 0.0, DT * b)
                    yl, yh = [], []
                    for i, k in enumerate(YK):
                        l = so[k, h, x + 1, pl.ds(7 + 8 * g, 8), :]
                        r = so[k, h, x + 1, pl.ds(9 + 8 * g, 8), :]
                        if g == 0:
                            e = jnp.broadcast_to(go[i, 0, h, pl.ds(x, 1), :], (8, 128))
                            l = jnp.where(first, e, l)
                        else:
                            e = jnp.broadcast_to(go[i, 1, h, pl.ds(x, 1), :], (8, 128))
                            r = jnp.where(last, e, r)
                        yl.append(l)
                        yh.append(r)
                    for c in range(5):
                        d = so[XF[c], h, x + 2, mid, :] - so[XF[c], h, x, mid, :]
                        d = d + (yh[c] - yl[c])
                        r = rzo[h, c, rows, :] - 0.5 * d
                        if c:
                            k = VF[c - 1]
                            s = so[k, h, x + 2, mid, :] + so[k, h, x, mid, :]
                            s = s + (yh[4 + c] + yl[4 + c])
                            r = r + (0.8 * s - 3.2 * so[k, h, x + 1, mid, :])
                        v = ch * r + (u[h, c, rows, :] if b == 1.0 else b * u[h, c, rows, :])
                        if a:
                            v = v + a * u0o[h, c, rows, :]
                        uo[h, c, rows, :] = v
            return 0

        lax.fori_loop(0, 32, body, 0, unroll=2)

    def near_p(u):
        def body(i, _):
            s = i // 8
            n = lax.rem(i, 8)
            for ch in range(2):
                rows = pl.ds(pl.multiple_of(n * 64 + ch * 32, 32), 32)
                w = [u[s, c, rows, :] for c in range(5)]
                rho, mx, my, mz, en = w
                vx, vy, vz, p, q, h = primitives(w)
                txz, tyz = mx * vz, my * vz
                vals = {
                    TXX: mx * vx + p, TXY: mx * vy, TXZ: txz, TYY: my * vy + p, TYZ: tyz,
                    HX: h * vx, HY: h * vy, VX: vx, VY: vy, VZ: vz, Q: q, MX: mx, MY: my,
                }
                for k, v in vals.items():
                    sn[k, s, n, pl.ds(8 + ch * 32, 32), :] = v
                flux = jnp.concatenate([mz, txz, tyz, mz * vz + p, h * vz], axis=0).astype(BF16)
                visc = jnp.concatenate([vx, vy, vz, q], axis=0).astype(BF16)
                df = jnp.dot(flux, znear[0], preferred_element_type=F32)
                sf = jnp.dot(visc, znear[1], preferred_element_type=F32)
                gz = met[s, 2, rows, :]
                gz2 = 0.8 * gz * gz
                for c in range(5):
                    r = gz * df[32 * c : 32 * c + 32]
                    if c:
                        r = r + gz2 * sf[32 * c - 32 : 32 * c]
                    rzn[s, c, rows, :] = r
            return 0

        lax.fori_loop(0, 8 * BCAP, body, 0, unroll=2)

    def near_ghosts(st):
        for s in range(BCAP):
            for side, base in ((0, S_LO), (1, S_HI)):
                row = tab[base + s]
                w = [
                    precv[st][row, s, c].astype(F32)[8 * side : 8 * side + 8] for c in range(5)
                ]
                for i, v in enumerate(y_terms(w)):
                    gn[i, side, s] = v

    def near_r(st, u, a, b, final):
        first = lax.broadcasted_iota(jnp.int32, (8, 128), 0) == 0
        last = lax.broadcasted_iota(jnp.int32, (8, 128), 0) == 7

        def cells(s, n, groups, keep):
            nm = jnp.maximum(n - 1, 0)
            np_ = jnp.minimum(n + 1, 7)
            sign = jnp.where(n == 0, -1.0, 1.0)
            for qd in groups:
                mid = pl.ds(8 + 8 * qd, 8)
                rows = pl.ds(pl.multiple_of(n * 64 + 8 * qd, 8), 8)
                ch = jnp.where(tab[S_NEAR + s * 8 + qd] >= 0, 0.0, DT * b)
                gxm, gym = met[s, 0, rows, :], met[s, 1, rows, :]
                hx, hy = -0.5 * gxm, -0.5 * gym
                gx2, gy2 = 0.8 * gxm * gxm, 0.8 * gym * gym
                yl, yh = [], []
                for i, k in enumerate(YK):
                    l = sn[k, s, n, pl.ds(7 + 8 * qd, 8), :]
                    r = sn[k, s, n, pl.ds(9 + 8 * qd, 8), :]
                    if qd == 0:
                        e = jnp.broadcast_to(gn[i, 0, s, pl.ds(n, 1), :], (8, 128))
                        l = jnp.where(first, e, l)
                    if qd == 7:
                        e = jnp.broadcast_to(gn[i, 1, s, pl.ds(n, 1), :], (8, 128))
                        r = jnp.where(last, e, r)
                    yl.append(l)
                    yh.append(r)
                for c in range(5):
                    lo = sn[XF[c], s, nm, mid, :]
                    if c in (0, 4):
                        lo = sign * lo
                    r = rzn[s, c, rows, :] + hx * (sn[XF[c], s, np_, mid, :] - lo)
                    r = r + hy * (yh[c] - yl[c])
                    if c:
                        k = VF[c - 1]
                        f2 = sn[k, s, n, mid, :]
                        f2 = f2 + f2
                        lo = sn[k, s, nm, mid, :]
                        if c < 4:
                            lo = sign * lo
                        r = r + gx2 * (sn[k, s, np_, mid, :] + lo - f2)
                        r = r + gy2 * (yh[4 + c] + yl[4 + c] - f2)
                    v = ch * r + (u[s, c, rows, :] if b == 1.0 else b * u[s, c, rows, :])
                    if a:
                        v = v + a * u0n[s, c, rows, :]
                    if final:
                        v = jnp.where(keep, v, 0.0)
                    un[s, c, rows, :] = v

        def edges(n, _):
            for s in range(BCAP):
                cells(s, n, (0, 7), tab[S_OCC + s] > 0)
            return 0

        def middle(s):
            keep = tab[S_OCC + s] > 0

            def body(n, _):
                cells(s, n, range(1, 7), keep)
                return 0

            lax.fori_loop(0, 8, body, 0)

        lax.fori_loop(0, 8, edges, 0)
        if not final:
            send_faces(st + 1, un)
        outs = []
        for s in range(BCAP):
            middle(s)
            if s == 0 and not final:
                send_parcels(st + 1)
            if final:
                outs.append(pltpu.make_async_copy(un.at[s], near_out.at[s], out_sem.at[2 + s]))
                outs[-1].start()
        return outs

    def off_section(st):
        u = uo if st else u0o
        for c in halo_copies(st, u):
            c.wait_send()
            c.wait_recv()
        off_ghosts(st)
        off_r(u, *RK[st])
        if st < 2:
            send_halos(st + 1, uo)

    def near_section(st):
        finish_faces(st)
        near_ghosts(st)
        return near_r(st, un if st else u0n, *RK[st], st == 2)

    lax.fori_loop(0, NT_OFF, settle_off, 0)
    send_halos(0, u0o)
    start_rows(1, 0)
    start_rows(1, 4)
    off_p(u0o)
    off_section(0)
    start_rows(1, 8)
    start_rows(1, 12)
    off_p(uo)
    off_section(1)
    off_p(uo)
    finish_rows(1)
    lax.fori_loop(0, NT_NEAR, settle_near, 0)
    send_faces(0, u0n)
    near_p(u0n)
    send_parcels(0)
    off_section(2)
    oc = [
        pltpu.make_async_copy(uo.at[h], off_out.at[:, :, pl.ds(128 * h, 128)], out_sem.at[h])
        for h in range(2)
    ]
    for c in oc:
        c.start()
    near_section(0)
    near_p(un)
    near_section(1)
    near_p(un)
    outs = near_section(2)
    for c in oc + outs:
        c.wait()


def advance(fin, fout, slot, faces, off, near, metric, maps_in, maps_out, zoff, znear):
    dma = pltpu.SemaphoreType.DMA
    return pl.pallas_call(
        main_kernel,
        out_shape=(
            jax.ShapeDtypeStruct((5, 512, 256), F32),
            jax.ShapeDtypeStruct((BCAP, 5, 512, 128), F32),
        ),
        in_specs=[pl.BlockSpec(memory_space=pltpu.SMEM)] * 4
        + [pl.BlockSpec(memory_space=pl.ANY)] * 7,
        out_specs=(pl.BlockSpec(memory_space=pl.ANY), pl.BlockSpec(memory_space=pl.ANY)),
        scratch_shapes=[
            pltpu.VMEM((2, 5, 512, 128), F32),
            pltpu.VMEM((BCAP, 5, 512, 128), F32),
            pltpu.VMEM((2, 5, 512, 128), F32),
            pltpu.VMEM((BCAP, 5, 512, 128), F32),
            pltpu.VMEM((BCAP, 3, 512, 128), F32),
            pltpu.VMEM((13, 2, 34, 32, 128), F32),
            pltpu.VMEM((13, BCAP, 8, 80, 128), F32),
            pltpu.VMEM((2, 5, 512, 128), F32),
            pltpu.VMEM((BCAP, 5, 512, 128), F32),
            pltpu.VMEM((NROW, 128, 128), BF16),
            pltpu.VMEM((NROW, 128, 128), BF16),
            pltpu.VMEM((2, 256, 256), BF16),
            pltpu.VMEM((2, 128, 128), BF16),
            pltpu.VMEM((PEERS, 320, 128), BF16),
            pltpu.VMEM((PEERS, 320, 128), BF16),
            pltpu.VMEM((PEERS, 320, 128), BF16),
            pltpu.VMEM((PEERS, 320, 128), BF16),
            pltpu.VMEM((8, 128), jnp.int32),
            pltpu.VMEM((PEERS, 8, 128), jnp.int32),
            pltpu.VMEM((3, BCAP, 5, 16, 128), BF16),
            pltpu.VMEM((4, BCAP, 5, 16, 128), BF16),
            pltpu.VMEM((4, BCAP, 5, 16, 128), BF16),
            pltpu.VMEM((4, BCAP, 5, 16, 128), BF16),
            pltpu.VMEM((3, 4, BCAP, 5, 16, 128), BF16),
            pltpu.VMEM((4, BCAP, 5, 16, 128), BF16),
            pltpu.VMEM((4, BCAP, 5, 16, 128), BF16),
            pltpu.VMEM((4, BCAP, 5, 16, 128), BF16),
            pltpu.VMEM((3, 2, 2, 5, 16, 128), F32),
            pltpu.VMEM((3, 2, 2, 5, 32, 128), BF16),
            pltpu.VMEM((3, 2, 2, 5, 32, 128), BF16),
            pltpu.VMEM((9, 2, 2, 32, 128), F32),
            pltpu.VMEM((9, 2, BCAP, 8, 128), F32),
            pltpu.SMEM((PEERS, 8, 128), jnp.int32),
            pltpu.SMEM((80,), jnp.int32),
            dma((9,)),
            dma((5,)),
            dma((PEERS,)),
            dma((PEERS,)),
            dma((2, PEERS)),
            dma((2, PEERS)),
            dma((3, 4)),
            dma((3, 4)),
            dma((3, 4)),
            dma((3, 4)),
            dma((3, 2)),
            dma((3, 2)),
            dma((3, 2)),
            dma((3, 2)),
        ],
        compiler_params=pltpu.CompilerParams(
            collective_id=0, has_side_effects=True, vmem_limit_bytes=67043328
        ),
        name="advance",
    )(fin, fout, slot, faces, off, near, metric, maps_in, maps_out, zoff, znear)


def z_matrices(width, wrap):
    col = np.arange(width)
    up, down = np.roll(col, -1), np.roll(col, 1)
    if not wrap:
        up[-1], down[0] = width - 1, 0
    first, second = np.zeros((2, width, width), np.float32)
    scale = 0.5 if wrap else 1.0
    for c in range(width):
        first[up[c], c] -= 0.5
        first[down[c], c] += 0.5
        second[up[c], c] += scale
        second[down[c], c] += scale
        second[c, c] -= 2.0 * scale
    return jnp.asarray(np.stack([first, second]), BF16)


def local(
    off_state,
    near_state,
    near_metric,
    slot_block,
    block_faces,
    fringe_in,
    fringe_in_maps,
    fringe_out,
    fringe_out_maps,
):
    off_next, near_next = advance(
        fringe_in,
        fringe_out,
        slot_block,
        block_faces.T,
        off_state.reshape(5, 512, 256),
        near_state.reshape(BCAP, 5, 512, 128),
        near_metric.reshape(BCAP, 3, 512, 128),
        fringe_in_maps,
        fringe_out_maps,
        z_matrices(256, True),
        z_matrices(128, False),
    )
    return off_next.reshape(off_state.shape), near_next.reshape(near_state.shape)


def solution(mesh):
    in_specs = (
        P(None, "gx", "gy", None),
        P(("gx", "gy"), None, None, None, None),
        P(("gx", "gy"), None, None, None, None),
        P(("gx", "gy")),
        P(),
        P(None, ("gx", "gy")),
        P(("gx", "gy"), None, None),
        P(None, ("gx", "gy")),
        P(("gx", "gy"), None, None),
    )
    out_specs = (P(None, "gx", "gy", None), P(("gx", "gy"), None, None, None, None))
    return jax.shard_map(local, mesh=mesh, in_specs=in_specs, out_specs=out_specs, check_vma=False)
```
